512 devices in a mesh: ctx: 128 (over y, z, core), head: 4 (over x).
Axes of the slice: x: 4, y: 4, z: 16, core: 2. Of those that a mesh axis runs over, the one named last changes fastest.
Arguments:
- branch_q: bfloat16 [16384, 4, 1024], P('ctx', 'head'), may hold values from -6 to 6
- branch_k: bfloat16 [16384, 4, 128], P('ctx', 'head'), may hold values from -6 to 6
- branch_v: bfloat16 [16384, 4, 128], P('ctx', 'head'), may hold values from -6 to 6
- branch_o: bfloat16 [16384, 4, 1024], P('ctx', 'head'), may hold values from -4 to 4
- branch_dout: bfloat16 [16384, 4, 1024], P('ctx', 'head'), may hold values from -512 to 512
- prompt_q: bfloat16 [256, 4, 1024], P('ctx', 'head'), may hold values from -6 to 6
- prompt_k: bfloat16 [256, 4, 128], P('ctx', 'head'), may hold values from -6 to 6
- prompt_v: bfloat16 [256, 4, 128], P('ctx', 'head'), may hold values from -6 to 6
- prompt_o: bfloat16 [256, 4, 1024], P('ctx', 'head'), may hold values from -4 to 4
- prompt_dout: bfloat16 [256, 4, 1024], P('ctx', 'head'), may hold values from -512 to 512
- gains: float32 [2, 128], replicated, may hold values from 0.8 to 2
- parents: int32 [128], P('ctx'), may hold values from 0 to 128, as said below
- depth: int32 [16384], P('ctx'), may hold values from 128 to 1279, as said below
Outputs:
- branch_dq: bfloat16 [16384, 4, 1024], P('ctx', 'head')
- branch_dk: bfloat16 [16384, 4, 128], P('ctx', 'head')
- branch_dv: bfloat16 [16384, 4, 128], P('ctx', 'head')
- prompt_dq: bfloat16 [256, 4, 1024], P('ctx', 'head')
- prompt_dk: bfloat16 [256, 4, 128], P('ctx', 'head')
- prompt_dv: bfloat16 [256, 4, 128], P('ctx', 'head')
- gain_grads: float32 [2, 128], replicated
The draws below stay inside these ranges and needn't reach their ends.
Inputs may be any that keep to these rules, and one draw needn't show every extreme that they name: `parents`: the parent of a branch block is a prompt block or an earlier branch block of the same subtree. A subtree is a run of consecutive branch blocks whose first block's parent is a prompt block; a run has at most 8 blocks, and some run has exactly 8. depth of a branch token = 128 times the number of its block's proper ancestor blocks, prompt blocks up to the fork included, plus its offset in its block.
All inputs are finite; a program needn't handle non-finite values.
Results may differ from the reference program's by a relative error of at most 0.0093.
Values may be sent and summed in bfloat16 or wider, within the bound.
A program may use at most 64 MiB of HBM per device.

```python
import jax
import jax.numpy as jnp
from jax import lax

HD = 128
G = 8
BLK = 128
SUB = 8
PFX = 256
KVH = 4
NTOK = 16384


DOUT_SCALE = 8.0


def tree_tables(base_key):
    block_count = NTOK // BLK
    prompt_blocks = PFX // BLK
    split_keys = jax.random.split(jax.random.fold_in(base_key, 11), 5)
    start_coin = jax.random.randint(split_keys[0], (block_count,), 0, 3, dtype=jnp.int32)
    full_start = block_count - SUB
    fork_draw = jax.random.randint(split_keys[2], (block_count,), 0, prompt_blocks, dtype=jnp.int32)
    pick_draw = jax.random.randint(split_keys[3], (block_count,), 0, 1 << 20, dtype=jnp.int32)
    keep_chain = jax.random.randint(split_keys[4], (block_count,), 0, 2, dtype=jnp.int32)

    def step(carries, block_index):
        root_block, run_length, depth_starts = carries
        inside = block_index > full_start
        outside = jnp.logical_not(inside)
        fresh = (block_index == 0) | (block_index == full_start) | (run_length >= SUB) & outside | (start_coin[block_index] == 0) & outside
        root_block = jnp.where(fresh, block_index, root_block)
        run_length = jnp.where(fresh, 1, run_length + 1)
        span_back = jnp.maximum(block_index - root_block, 1)
        earlier = root_block + pick_draw[block_index] % span_back
        inner = jnp.where((keep_chain[block_index] == 1) | inside, block_index - 1, earlier)
        inner_safe = jnp.clip(inner, 0, block_count - 1)
        fork_value = jnp.where(block_index == full_start, prompt_blocks - 1, fork_draw[block_index])
        parent = jnp.where(fresh, fork_value, prompt_blocks + inner)
        begin = jnp.where(fresh, BLK * (fork_value + 1), depth_starts[inner_safe] + BLK)
        depth_starts = depth_starts.at[block_index].set(begin)
        return ((root_block, run_length, depth_starts), parent)
    start_state = (jnp.zeros((), jnp.int32), jnp.zeros((), jnp.int32), jnp.zeros((block_count,), jnp.int32))
    finals, parent_list = lax.scan(step, start_state, jnp.arange(block_count, dtype=jnp.int32))
    depth_starts = finals[2]
    depth_values = (depth_starts[:, None] + jnp.arange(BLK, dtype=jnp.int32)[None, :]).reshape(block_count * BLK)
    return (parent_list.astype(jnp.int32), depth_values.astype(jnp.int32))


def draw_parents(key, part):
    return tree_tables(key)[0]


def draw_depth(key, part):
    return tree_tables(key)[1]


def rising(base_key, row_count):
    array_shape = (row_count, KVH, G * HD)
    row_index = jnp.arange(row_count, dtype=jnp.float32) / max(row_count - 1, 1)
    head_rise = 1.0 + 2.0 * jnp.arange(KVH, dtype=jnp.float32) / max(KVH - 1, 1)
    noise_part = jax.random.truncated_normal(base_key, -5.0, 5.0, array_shape, jnp.float32)
    row_rise = 1.0 + 2.0 * row_index
    return (DOUT_SCALE * noise_part * row_rise[:, None, None] * head_rise[None, :, None]).astype(jnp.bfloat16)


def draw_branch_dout(key, part):
    return rising(jax.random.fold_in(key, 21), NTOK)


def draw_prompt_dout(key, part):
    return rising(jax.random.fold_in(key, 22), PFX)


def block_levels(own_key, extent, shards, smallest, largest):
    level = 1.0
    for dim, parts in shards:
        heights = jax.random.uniform(jax.random.fold_in(jax.random.fold_in(own_key, 6), dim), (parts,), jnp.float32, smallest / len(shards), largest / len(shards))
        level = level * jnp.repeat(jnp.exp(heights), extent[dim] // parts).reshape((-1,) + (1,) * (len(extent) - 1 - dim))
    return level


def bell_draw(own_key, dims, width, bound, cuts=(), held_as=jnp.bfloat16):
    values = width * jax.random.normal(own_key, dims, jnp.float32)
    if cuts:
        values = values * block_levels(own_key, dims, cuts, -0.22, 0.18)
    return jnp.clip(values, -bound, bound).astype(held_as)


def setup_inputs(seed: int = 0) -> dict:
    key_list = jax.random.split(jax.random.key(seed), 14)
    branch_q = bell_draw(key_list[0], (NTOK, KVH, G * HD), 1.0, 6.0, ((0, 128), (1, 4)))
    branch_k = bell_draw(key_list[1], (NTOK, KVH, HD), 1.0, 6.0, ((0, 128), (1, 4)))
    branch_v = bell_draw(key_list[2], (NTOK, KVH, HD), 1.0, 6.0, ((0, 128), (1, 4)))
    branch_o = bell_draw(key_list[3], (NTOK, KVH, G * HD), 0.3, 4.0, ((0, 128), (1, 4)))
    branch_dout = draw_branch_dout(jax.random.fold_in(key_list[13], 71), 0)
    prompt_q = bell_draw(key_list[5], (PFX, KVH, G * HD), 1.0, 6.0, ((0, 128), (1, 4)))
    prompt_k = bell_draw(key_list[6], (PFX, KVH, HD), 1.0, 6.0, ((0, 128), (1, 4)))
    prompt_v = bell_draw(key_list[7], (PFX, KVH, HD), 1.0, 6.0, ((0, 128), (1, 4)))
    prompt_o = bell_draw(key_list[8], (PFX, KVH, G * HD), 0.3, 4.0, ((0, 128), (1, 4)))
    prompt_dout = draw_prompt_dout(jax.random.fold_in(key_list[13], 71), 0)
    gains = jnp.clip(jax.random.uniform(key_list[10], (2, HD), jnp.float32, 0.8, 2.0), 0.8, 2.0)
    parents = draw_parents(jax.random.fold_in(key_list[13], 71), 0)
    depth = draw_depth(jax.random.fold_in(key_list[13], 71), 0)
    return dict(branch_q=branch_q, branch_k=branch_k, branch_v=branch_v, branch_o=branch_o, branch_dout=branch_dout, prompt_q=prompt_q, prompt_k=prompt_k, prompt_v=prompt_v, prompt_o=prompt_o, prompt_dout=prompt_dout, gains=gains, parents=parents, depth=depth)


EPS = 1e-06
THETA = 1000000.0

def angles(positions, head_size):
    half_size = head_size // 2
    frequencies = THETA ** (-(jnp.arange(half_size, dtype=jnp.float32) * 2.0) / head_size)
    return positions.astype(jnp.float32)[:, None] * frequencies[None, :]

def rotate(values, angle_table):
    half_size = values.shape[-1] // 2
    cosine = jnp.cos(angle_table)
    sine_part = jnp.sin(angle_table)
    first_half = values[..., :half_size]
    second_half = values[..., half_size:]
    return jnp.concatenate([first_half * cosine - second_half * sine_part, second_half * cosine + first_half * sine_part], axis=-1)

def prepare(raw_values, gain_vector, angle_table):
    widened = raw_values.astype(jnp.float32)
    inverse = lax.rsqrt(lax.optimization_barrier(jnp.mean(widened * widened, axis=-1, keepdims=True)) + EPS)
    unit_values = widened * inverse
    rotated = rotate(unit_values * gain_vector, angle_table).astype(jnp.bfloat16)
    return (unit_values, inverse, rotated)

def norm_back(grad_rotated, unit_values, inverse, gain_vector, angle_table):
    grad_normed = rotate(grad_rotated, -angle_table)
    scaled = grad_normed * gain_vector
    grad_raw = (scaled - unit_values * lax.optimization_barrier(jnp.mean(scaled * unit_values, axis=-1, keepdims=True))) * inverse
    gain_part = lax.optimization_barrier(jnp.sum((grad_normed * unit_values).reshape(-1, unit_values.shape[-1]), axis=0))
    return (grad_raw, gain_part)

def attend_back(rotated_q, key_rows, value_rows, visible, grad_out, saved_out):
    query_wide = rotated_q.astype(jnp.float32)
    key_wide = key_rows.astype(jnp.float32)
    value_wide = value_rows.astype(jnp.float32)
    grad_wide = grad_out.astype(jnp.float32)
    scores = jnp.einsum('rgd,kd->rgk', query_wide, key_wide) * HD ** (-0.5)
    shown_mask = visible[:, None, :]
    totals = lax.optimization_barrier(jnp.sum(jnp.where(shown_mask, jnp.exp(scores), 0.0), axis=-1, keepdims=True))
    weights = jnp.where(shown_mask, jnp.exp(scores - jnp.log(totals)), 0.0)
    weight_half = lax.optimization_barrier(weights.astype(jnp.bfloat16)).astype(jnp.float32)
    row_delta = lax.optimization_barrier(jnp.sum(grad_wide * saved_out.astype(jnp.float32), axis=-1, keepdims=True))
    grad_v = jnp.einsum('rgk,rgd->kd', weight_half, grad_wide)
    grad_p = jnp.einsum('rgd,kd->rgk', grad_wide, value_wide)
    grad_s = lax.optimization_barrier((weights * (grad_p - row_delta)).astype(jnp.bfloat16)).astype(jnp.float32)
    grad_q = jnp.einsum('rgk,kd->rgd', grad_s, key_wide) * HD ** (-0.5)
    grad_k = jnp.einsum('rgk,rgd->kd', grad_s, query_wide) * HD ** (-0.5)
    return (grad_q, grad_k, grad_v)

def reference(branch_q, branch_k, branch_v, branch_o, branch_dout, prompt_q, prompt_k, prompt_v, prompt_o, prompt_dout, gains, parents, depth):
    block_count = NTOK // BLK
    prompt_blocks = PFX // BLK
    window_size = SUB * BLK
    padding = (SUB - 1) * BLK
    gain_q = gains[0]
    gain_k = gains[1]
    angle_branch = angles(depth, HD)
    prompt_ids = jnp.arange(PFX, dtype=jnp.int32)
    angle_prompt = angles(prompt_ids, HD)
    unit_bk, inverse_bk, rotated_bk = prepare(branch_k, gain_k, angle_branch[:, None, :])
    unit_pk, inverse_pk, rotated_pk = prepare(prompt_k, gain_k, angle_prompt[:, None, :])
    keys_padded = jnp.concatenate([jnp.zeros((padding, KVH, HD), jnp.bfloat16), rotated_bk])
    values_padded = jnp.concatenate([jnp.zeros((padding, KVH, HD), jnp.bfloat16), branch_v])
    key_ids = jnp.arange(window_size, dtype=jnp.int32)
    key_slot = key_ids // BLK
    key_offset = key_ids % BLK
    row_offset = jnp.arange(BLK, dtype=jnp.int32)
    slot_ids = jnp.arange(SUB, dtype=jnp.int32)
    causal = (key_slot[None, :] != SUB - 1) | (key_offset[None, :] <= row_offset[:, None])
    attend = jax.vmap(attend_back, in_axes=(1, 1, 1, None, 1, 1), out_axes=(1, 1, 1))

    def block_step(carries, block_index):
        grad_kb, grad_vb, grad_kp, grad_vp = carries
        start_row = block_index * BLK

        def climb(step_index, climb_state):
            current, ancestors, fork_block = climb_state
            branchy = current >= prompt_blocks
            located = current - prompt_blocks - (block_index - SUB + 1)
            matched = (slot_ids == located) & branchy
            upward = parents[jnp.clip(current - prompt_blocks, 0, block_count - 1)].astype(jnp.int32)
            return (jnp.where(branchy, upward, current), ancestors | matched, jnp.where(branchy, fork_block, current))
        start_state = (block_index + prompt_blocks, jnp.zeros((SUB,), dtype=bool), jnp.zeros((), jnp.int32))
        unused, ancestors, fork_block = lax.fori_loop(0, SUB + 1, climb, start_state)
        prompt_seen = jnp.broadcast_to((prompt_ids < BLK * (fork_block + 1))[None, :], (BLK, PFX))
        window_seen = ancestors[key_slot][None, :] & causal
        visible = jnp.concatenate([prompt_seen, window_seen], axis=1)
        key_rows = jnp.concatenate([rotated_pk, lax.dynamic_slice_in_dim(keys_padded, start_row, window_size, 0)])
        value_rows = jnp.concatenate([prompt_v, lax.dynamic_slice_in_dim(values_padded, start_row, window_size, 0)])
        angle_block = lax.dynamic_slice_in_dim(angle_branch, start_row, BLK, 0)[:, None, None, :]
        queries = lax.dynamic_slice_in_dim(branch_q, start_row, BLK, 0).reshape(BLK, KVH, G, HD)
        unit_q, inverse_q, rotated_q = prepare(queries, gain_q, angle_block)
        grad_out = lax.dynamic_slice_in_dim(branch_dout, start_row, BLK, 0).reshape(BLK, KVH, G, HD)
        saved_out = lax.dynamic_slice_in_dim(branch_o, start_row, BLK, 0).reshape(BLK, KVH, G, HD)
        grad_q, grad_k, grad_v = attend(rotated_q, key_rows, value_rows, visible, grad_out, saved_out)
        raw_q, gain_part = norm_back(grad_q, unit_q, inverse_q, gain_q, angle_block)
        window_k = lax.dynamic_slice_in_dim(grad_kb, start_row, window_size, 0) + grad_k[PFX:]
        window_v = lax.dynamic_slice_in_dim(grad_vb, start_row, window_size, 0) + grad_v[PFX:]
        grad_kb = lax.dynamic_update_slice_in_dim(grad_kb, window_k, start_row, 0)
        grad_vb = lax.dynamic_update_slice_in_dim(grad_vb, window_v, start_row, 0)
        outcome = (grad_kb, grad_vb, grad_kp + grad_k[:PFX], grad_vp + grad_v[:PFX])
        return (outcome, (raw_q.reshape(BLK, KVH, G * HD).astype(jnp.bfloat16), gain_part))
    zeros_branch = jnp.zeros((padding + NTOK, KVH, HD), jnp.float32)
    zeros_prompt = jnp.zeros((PFX, KVH, HD), jnp.float32)
    carries, stacked = lax.scan(block_step, (zeros_branch, zeros_branch, zeros_prompt, zeros_prompt), jnp.arange(block_count, dtype=jnp.int32))
    grad_kb, grad_vb, grad_kp, grad_vp = carries
    branch_dq = stacked[0].reshape(NTOK, KVH, G * HD)
    angle_rows = angle_prompt[:, None, None, :]
    unit_pq, inverse_pq, rotated_pq = prepare(prompt_q.reshape(PFX, KVH, G, HD), gain_q, angle_rows)
    prompt_visible = prompt_ids[None, :] <= prompt_ids[:, None]
    grad_pq, grad_pk, grad_pv = attend(rotated_pq, rotated_pk, prompt_v, prompt_visible, prompt_dout.reshape(PFX, KVH, G, HD), prompt_o.reshape(PFX, KVH, G, HD))
    raw_pq, gain_pq = norm_back(grad_pq, unit_pq, inverse_pq, gain_q, angle_rows)
    raw_bk, gain_bk = norm_back(grad_kb[padding:], unit_bk, inverse_bk, gain_k, angle_branch[:, None, :])
    raw_pk, gain_pk = norm_back(grad_kp + grad_pk, unit_pk, inverse_pk, gain_k, angle_prompt[:, None, :])
    sum_q = lax.optimization_barrier(jnp.sum(stacked[1], axis=0)) + gain_pq
    sum_k = gain_bk + gain_pk
    gain_grads = jnp.stack([sum_q * ((NTOK + PFX) * KVH * G) ** (-0.5), sum_k * ((NTOK + PFX) * KVH) ** (-0.5)])
    return (branch_dq, raw_bk.astype(jnp.bfloat16), grad_vb[padding:].astype(jnp.bfloat16), raw_pq.reshape(PFX, KVH, G * HD).astype(jnp.bfloat16), raw_pk.astype(jnp.bfloat16), (grad_vp + grad_pv).astype(jnp.bfloat16), gain_grads)
```

```python
import math

import numpy as np

import jax
import jax.numpy as jnp
from jax import lax
from jax.experimental import pallas as pl
from jax.experimental.pallas import tpu as pltpu
from jax.sharding import PartitionSpec as P

HD = 128
G = 8
BLK = 128
SUB = 8
PFX = 256
EPS = 1e-06
THETA = 1000000.0
Y = 4
Z = 16
GRP = 2 * Y
X = 4
NCTX = Y * Z * 2
ROWS = BLK * G
PROWS = 128
ALLR = ROWS + PROWS
KEYS = PFX + SUB * BLK
SCALE = HD ** (-0.5)
EXP2_SCALE = SCALE * math.log2(math.e)
MESH = pl.DeviceIdType.MESH
F32 = jnp.float32
BF16 = jnp.bfloat16


def prompt_order():
    p = np.arange(PFX)
    return (p // 4 % 4) * 64 + (p // 16) * 4 + p % 4


def tables():
    freq = THETA ** (-(np.arange(HD // 2, dtype=np.float64) * 2.0) / HD)

    def pair(positions):
        angle = positions[:, None].astype(np.float64) * freq[None, :]
        cosine, sine = np.cos(angle), np.sin(angle)
        return np.stack(
            [np.concatenate([cosine, cosine], 1), np.concatenate([-sine, sine], 1)]
        ).astype(np.float32)

    offset = pair(np.arange(BLK))
    level = pair(np.arange(16) * BLK)
    prompt = pair(prompt_order())
    return offset, level, prompt


def norm(x):
    inverse = lax.rsqrt(jnp.mean(x * x, axis=-1, keepdims=True) + EPS)
    return x * inverse, inverse


def swap(x):
    return pltpu.roll(x, HD // 2, 1)


def rotate(x, c, s):
    return x * c + swap(x) * s


def unrotate(x, c, s):
    return x * c - swap(x) * s


def norm_back(grad, unit, inverse, gain, c, s):
    g = unrotate(grad, c, s)
    u = g * gain
    raw = (u - unit * jnp.mean(u * unit, axis=-1, keepdims=True)) * inverse
    return raw, jnp.sum(g * unit, axis=0, keepdims=True)


def nt(a, b):
    return lax.dot_general(a, b, (((1,), (1,)), ((), ())), preferred_element_type=F32)


def nn(a, b):
    return lax.dot_general(a, b, (((1,), (0,)), ((), ())), preferred_element_type=F32)


def kernel(
    q_ref, k_hbm, v_hbm, o_ref, do_ref, pq_ref, pk_ref, pv_ref, po_ref, pdo_ref,
    gains_ref, par_ref, depth_ref, toff_ref, tlev_ref, tpr_ref,
    dq_ref, dk_ref, dv_ref, pdq_ref, pdk_ref, pdv_ref, gg_ref,
    kv, parw, grp, pkv,
    qrot, qunit, qinv, dor, delta, krot, krott, kunit, kinv, ctab, stab, thr, e_s, tot, dqt,
    scr, pscr, vp,
    wterm, ownk, ownv, prx, mtx, mrx, pterm, rs1, rs2t, rs2, g1, g2,
    s_loc, s_kv, r_kv, s_par, r_par, s_ag1, r_ag1, s_ag2, r_ag2,
    s_p, r_p, s_m, r_m, s_rs1, r_rs1, s_rs2, r_rs2, s_g1, r_g1, s_g2, r_g2,
):
    me = lax.axis_index("ctx")
    hx = lax.axis_index("head")
    y = me // (2 * Z)
    z = lax.rem(me // 2, Z)
    c = lax.rem(me, 2)
    gi = y * 2 + c
    partner = me + 1 - 2 * c
    base = gi * 2

    def at(offset):
        return lax.rem(me + (offset + NCTX), NCTX)

    def grp_dev(index):
        return ((index // 2) * Z + z) * 2 + lax.rem(index, 2)

    def z_dev(index):
        return (y * Z + index) * 2 + c

    def copy(src, dst, ssem, rsem, device, head=None):
        where = {"ctx": device} if head is None else {"ctx": device, "head": head}
        return pltpu.make_async_remote_copy(
            src_ref=src, dst_ref=dst, send_sem=ssem, recv_sem=rsem,
            device_id=where, device_id_type=MESH,
        )

    own = [
        pltpu.make_async_copy(k_hbm, kv.at[0, 0], s_loc.at[0]),
        pltpu.make_async_copy(v_hbm, kv.at[0, 1], s_loc.at[1]),
    ]
    for cp in own:
        cp.start()
    barrier = pltpu.get_barrier_semaphore()

    def greet(device, head=None):
        where = {"ctx": device} if head is None else {"ctx": device, "head": head}
        pl.semaphore_signal(barrier, inc=1, device_id=where, device_id_type=MESH)

    for offset in (-7, -6, -5, -4, -3, -2, -1, 1, 2):
        greet(at(offset))

    @pl.loop(1, Z)
    def _(j):
        greet(z_dev(lax.rem(z + j, Z)))

    @pl.loop(1, GRP * X)
    def _(j):
        other = lax.rem(hx * GRP + gi + j, GRP * X)
        greet(grp_dev(lax.rem(other, GRP)), other // GRP)

    parw[0] = jnp.full((1, HD), par_ref[0], jnp.int32)
    row16 = lax.broadcasted_iota(jnp.int32, (16, HD), 0)

    def spread(two_rows):
        x = two_rows.astype(F32)
        first = jnp.broadcast_to(x[0:1], (16, HD))
        second = jnp.broadcast_to(x[1:2], (16, HD))
        return jnp.where(row16 == base, first, jnp.where(row16 == base + 1, second, 0.0))

    grp[gi, 0:16, :] = spread(pk_ref[...]).astype(BF16)
    grp[gi, 16:32, :] = spread(pv_ref[...]).astype(BF16)

    gain_q = gains_ref[0:1, :]
    gain_k = gains_ref[1:2, :]
    lane1 = lax.broadcasted_iota(jnp.int32, (1, HD), 1)
    level = (depth_ref[...] - lane1) >> 7

    def level_rows(lv):
        cl = jnp.zeros((1, HD), F32)
        sl = jnp.zeros((1, HD), F32)
        for n in range(1, SUB + 2):
            cl = jnp.where(lv == n, tlev_ref[0, n : n + 1, :], cl)
            sl = jnp.where(lv == n, tlev_ref[1, n : n + 1, :], sl)
        return cl, sl

    def block_tables(lv):
        cl, sl = level_rows(lv)
        co, so = toff_ref[0], toff_ref[1]
        return co * cl - so * sl, so * cl + co * sl

    c0, s0 = block_tables(level)
    ctab[0] = c0
    stab[0] = s0

    @pl.loop(0, G)
    def _(g):
        lanes = pl.ds(pl.multiple_of(g * HD, HD), HD)
        rows = pl.ds(pl.multiple_of(g * BLK, BLK), BLK)
        unit, inverse = norm(q_ref[:, lanes].astype(F32))
        qunit[rows, :] = unit
        qinv[rows, :] = jnp.broadcast_to(inverse, (BLK, HD))
        qrot[rows, :] = rotate(unit * gain_q, ctab[0], stab[0]).astype(BF16)
        d = do_ref[:, lanes]
        dor[rows, :] = d
        prod = d.astype(F32) * o_ref[:, lanes].astype(F32)
        delta[:, lanes] = jnp.sum(prod.T, axis=0, keepdims=True)

    def to_rows(ref):
        x = ref[...].astype(F32)
        for g in range(G):
            scr[2 * g : 2 * g + 2, :] = x[:, g * HD : (g + 1) * HD]
        return scr[0:16, :]

    pslot = z * 16 + base
    odd = lax.rem(row16, 2) == 1

    def prow(n):
        first = jnp.broadcast_to(tpr_ref[n, pl.ds(pslot, 1), :], (16, HD))
        second = jnp.broadcast_to(tpr_ref[n, pl.ds(pslot + 1, 1), :], (16, HD))
        return jnp.where(odd, second, first)

    pc16, ps16 = prow(0), prow(1)
    prest = pl.ds(ROWS + 16, PROWS - 16)
    punit, pinverse = norm(to_rows(pq_ref))
    qrot[ROWS : ROWS + 16, :] = rotate(punit * gain_q, pc16, ps16).astype(BF16)
    qrot[prest, :] = jnp.zeros((PROWS - 16, HD), BF16)
    pd = to_rows(pdo_ref)
    dor[ROWS : ROWS + 16, :] = pd.astype(BF16)
    dor[prest, :] = jnp.zeros((PROWS - 16, HD), BF16)
    pscr[...] = jnp.zeros((PROWS, HD), F32)
    pscr[0:16, :] = pd * to_rows(po_ref)
    delta[:, ROWS:] = jnp.sum(pscr[...].T, axis=0, keepdims=True)
    for cp in own:
        cp.wait()
    pl.semaphore_wait(barrier, 9 + (Z - 1) + (GRP * X - 1))

    def kv_copy(op, n, src, dst, device):
        return copy(kv.at[src, n], kv.at[dst, n], s_kv.at[op, n], r_kv.at[dst, n], device)

    def kv_arrived(slot, n):
        copy(kv.at[slot, n], kv.at[slot, n], s_kv.at[0, n], r_kv.at[slot, n], partner).wait_recv()

    sent = []

    def send(cp):
        cp.start()
        sent.append(cp)

    for n in range(2):
        send(kv_copy(0, n, 0, 2, at(2)))

    @pl.when(c == 0)
    def _():
        for n in range(2):
            kv_copy(1, n, 0, 1, partner).start()

    for j in range(1, GRP):
        send(copy(grp.at[gi], grp.at[gi], s_ag1.at[j], r_ag1.at[gi], grp_dev(lax.rem(gi + j, GRP))))
    for d in range(1, SUB):
        send(copy(parw.at[0], parw.at[d], s_par.at[d], r_par.at[d], at(d)))

    for n in range(2):
        kv_arrived(2, n)
        send(kv_copy(2, n, 2, 4, at(2)))
        send(kv_copy(3, n, 2, 3 - 2 * c, partner))
    for j in range(1, GRP):
        slot = lax.rem(gi + j, GRP)
        copy(grp.at[slot], grp.at[slot], s_ag1.at[j], r_ag1.at[slot], partner).wait_recv()
    tile = grp[0].astype(F32)
    for j in range(1, GRP):
        tile = tile + grp[j].astype(F32)
    pkv[z] = tile.astype(BF16)

    @pl.loop(1, Z)
    def _(j):
        copy(pkv.at[z], pkv.at[z], s_ag2.at[j], r_ag2.at[z], z_dev(lax.rem(z + j, Z))).start()

    for n in range(2):
        kv_arrived(4, n)
        send(kv_copy(4, n, 4, 6, at(2)))
        send(kv_copy(5, n, 4, 5 - 2 * c, partner))
    for n in range(2):
        kv_arrived(6, n)
        send(kv_copy(6, n, 6, 7, at(1)))

    @pl.when(c == 1)
    def _():
        for n in range(2):
            kv_copy(7, n, 6, 5, partner).start()

    for d in (1, 3, 5, 7):
        for n in range(2):
            kv_arrived(d, n)
    for d in range(1, SUB):
        copy(parw.at[d], parw.at[d], s_par.at[d], r_par.at[d], partner).wait_recv()

    @pl.loop(1, Z)
    def _(j):
        slot = lax.rem(z + j, Z)
        copy(pkv.at[slot], pkv.at[slot], s_ag2.at[j], r_ag2.at[slot], z_dev(slot)).wait_recv()

    block = me + PFX // BLK
    current = jnp.full((1, HD), block, jnp.int32)
    seen = [jnp.zeros((1, HD), jnp.int32) for _ in range(SUB)]
    levels = [jnp.zeros((1, HD), jnp.int32) for _ in range(SUB)]
    above = [parw[d] for d in range(SUB)]
    for step in range(SUB + 1):
        branchy = current >= PFX // BLK
        upward = jnp.zeros((1, HD), jnp.int32)
        for d in range(SUB):
            match = (current == block - d) & branchy
            seen[d] = jnp.where(match, 1, seen[d])
            levels[d] = jnp.where(match, level - step, levels[d])
            upward = jnp.where(match, above[d], upward)
        current = jnp.where(branchy, upward, current)
    fork = current

    def wide(x):
        return jnp.concatenate([x] * G, axis=1)

    thr[0] = jnp.where(wide(seen[0]) == 1, wide(lane1), -1)
    for d in range(1, SUB):
        thr[d] = jnp.where(wide(seen[d]) == 1, BLK, -1)
    thr_prompt = jnp.concatenate(
        [wide(BLK * (fork + 1) - 1), me * 2 + lax.rem(lane1, 2)], axis=1
    )

    pcos, psin = tpr_ref[0], tpr_ref[1]
    pk_all = jnp.concatenate([pkv[n, 0:16, :] for n in range(Z)], axis=0).astype(F32)
    for n in range(Z):
        vp[n * 16 : (n + 1) * 16, :] = pkv[n, 16:32, :]
    pkunit, _ = norm(pk_all)
    rot = rotate(pkunit * gain_k, pcos, psin)
    krot[0:PFX, :] = rot.astype(BF16)
    krott[:, 0:PFX] = rot.T.astype(BF16)
    kunit[0:PFX, :] = pkunit
    for d in range(SUB):
        rows = slice(PFX + d * BLK, PFX + (d + 1) * BLK)
        if d:
            cd, sd = block_tables(levels[d])
            ctab[d] = cd
            stab[d] = sd
        unit, inverse = norm(kv[d, 0].astype(F32))
        if d == 0:
            kinv[...] = jnp.broadcast_to(inverse, (BLK, HD))
        kunit[rows, :] = unit
        rot = rotate(unit * gain_k, ctab[d], stab[d])
        krot[rows, :] = rot.astype(BF16)
        krott[:, rows] = rot.T.astype(BF16)

    t_key = lax.broadcasted_iota(jnp.int32, (PFX, ALLR), 0)
    t_key = ((t_key >> 2) & 3) * 64 + (t_key >> 4) * 4 + (t_key & 3)
    s = nt(krot[0:PFX, :], qrot[...])
    e = jnp.where(t_key <= thr_prompt, jnp.exp2(s * EXP2_SCALE), 0.0)
    e_s[0:PFX, :] = e
    tot[...] = jnp.sum(e, axis=0, keepdims=True)
    offs = lax.broadcasted_iota(jnp.int32, (BLK, ROWS), 0)

    @pl.loop(0, SUB)
    def _(d):
        rows = pl.ds(pl.multiple_of(PFX + d * BLK, BLK), BLK)
        s = nt(krot[rows, :], qrot[0:ROWS, :])
        e = jnp.where(offs <= thr[d], jnp.exp2(s * EXP2_SCALE), 0.0)
        e_s[rows, 0:ROWS] = e
        tot[:, 0:ROWS] += jnp.sum(e, axis=0, keepdims=True)

    tot[...] = 1.0 / tot[...]

    def back(krows, vals, width):
        p = e_s[krows, 0:width] * tot[:, 0:width]
        d = dor[0:width, :]
        dv = nn(p.astype(BF16), d)
        dp = nt(vals, d)
        ds = (p * (dp - delta[:, 0:width])).astype(BF16)
        dk = nn(ds, qrot[0:width, :]) * SCALE
        return dk, dv, nn(krott[:, krows], ds)

    dk, dv, dqt0 = back(slice(0, PFX), vp[...], ALLR)
    dqt[...] = dqt0
    for n in range(Z):
        pterm[n, 0:16, :] = dk[n * 16 : (n + 1) * 16].astype(BF16)
        pterm[n, 16:32, :] = dv[n * 16 : (n + 1) * 16].astype(BF16)
    gk = jnp.sum(unrotate(dk, pcos, psin) * kunit[0:PFX, :], axis=0, keepdims=True)

    @pl.loop(1, Z)
    def _(j):
        other = lax.rem(z + j, Z)
        copy(pterm.at[other], rs1.at[z], s_rs1.at[j], r_rs1.at[z], z_dev(other)).start()

    for d in range(SUB - 1, -1, -1):
        rows = slice(PFX + d * BLK, PFX + (d + 1) * BLK)
        dk, dv, part = back(rows, kv[d, 1], ROWS)
        dqt[:, 0:ROWS] += part
        if d:
            wterm[d, 0] = dk.astype(BF16)
            wterm[d, 1] = dv.astype(BF16)
        else:
            ownk[...] = dk
            ownv[...] = dv
        gk = gk + jnp.sum(unrotate(dk, ctab[d], stab[d]) * kunit[rows, :], axis=0, keepdims=True)

    for n in range(2):
        send(copy(wterm.at[7, n], prx.at[3, n], s_p.at[3, n], r_p.at[3, n], at(-1)))
    for slot in (2, 1, 0):
        for n in range(2):
            send(copy(wterm.at[2 * slot + 1, n], prx.at[slot, n], s_p.at[slot, n], r_p.at[slot, n], partner))

    gq = jnp.zeros((1, HD), F32)
    for g in range(G):
        rows = slice(g * BLK, (g + 1) * BLK)
        grad = dqt[:, rows].T * SCALE
        raw, part = norm_back(grad, qunit[rows, :], qinv[rows, :], gain_q, ctab[0], stab[0])
        dq_ref[:, rows] = raw.astype(BF16)
        gq = gq + part
    grad = dqt[:, ROWS:].T[0:16] * SCALE
    raw, part = norm_back(grad, punit, pinverse, gain_q, pc16, ps16)
    gq = gq + part
    scr[...] = raw
    for g in range(G):
        pdq_ref[:, g * HD : (g + 1) * HD] = scr[2 * g : 2 * g + 2, :].astype(BF16)

    row8 = lax.broadcasted_iota(jnp.int32, (8, HD), 0)
    g1[z] = jnp.where(row8 == 0, gq, jnp.where(row8 == 1, gk, 0.0))

    @pl.loop(1, Z)
    def _(j):
        copy(g1.at[z], g1.at[z], s_g1.at[j], r_g1.at[z], z_dev(lax.rem(z + j, Z))).start()

    def p_arrived(slot, n):
        copy(prx.at[slot, n], prx.at[slot, n], s_p.at[slot, n], r_p.at[slot, n], partner).wait_recv()

    def m_arrived(k, n):
        copy(mrx.at[k, n], mrx.at[k, n], s_m.at[k, n], r_m.at[k, n], partner).wait_recv()

    for slot in range(4):
        for n in range(2):
            p_arrived(slot, n)
    for k in (3, 2, 1):
        for n in range(2):
            if k < 3:
                m_arrived(k, n)
            value = wterm[2 * k, n].astype(F32) + prx[k - c, n].astype(F32)
            if k == 3:
                value = value + jnp.where(c == 1, prx[3, n].astype(F32), 0.0)
            else:
                value = value + mrx[k, n].astype(F32)
            mtx[k - 1, n] = value.astype(BF16)
        for n in range(2):
            send(copy(mtx.at[k - 1, n], mrx.at[k - 1, n], s_m.at[k - 1, n], r_m.at[k - 1, n], at(-2)))
        if k == 3:

            @pl.loop(1, Z)
            def _(j):
                slot = lax.rem(z + j, Z)
                copy(rs1.at[slot], rs1.at[slot], s_rs1.at[j], r_rs1.at[slot], z_dev(slot)).wait_recv()

            rs1[z] = pterm[z]
            total = rs1[0].astype(F32)
            for n in range(1, Z):
                total = total + rs1[n].astype(F32)
            rs2[gi] = total.astype(BF16)
            for j in range(1, GRP):
                send(copy(rs2.at[gi], rs2.at[gi], s_rs2.at[j], r_rs2.at[gi], grp_dev(lax.rem(gi + j, GRP))))
        if k == 2:

            @pl.loop(1, Z)
            def _(j):
                slot = lax.rem(z + j, Z)
                copy(g1.at[slot], g1.at[slot], s_g1.at[j], r_g1.at[slot], z_dev(slot)).wait_recv()

            total = g1[0]
            for n in range(1, Z):
                total = total + g1[n]
            xg = hx * GRP + gi
            g2[xg] = total

            @pl.loop(1, GRP * X)
            def _(j):
                other = lax.rem(xg + j, GRP * X)
                copy(
                    g2.at[xg], g2.at[xg], s_g2.at[j], r_g2.at[xg], grp_dev(lax.rem(other, GRP)), other // GRP
                ).start()

    for n, total_ref in ((0, ownk), (1, ownv)):
        m_arrived(0, n)
        total_ref[...] += mrx[0, n].astype(F32)

        @pl.when(c == 0)
        def _():
            total_ref[...] += prx[0, n].astype(F32)

    raw, _ = norm_back(
        ownk[...], kunit[PFX : PFX + BLK, :], kinv[...], gain_k, ctab[0], stab[0]
    )
    dk_ref[...] = raw.astype(BF16)
    dv_ref[...] = ownv[...].astype(BF16)

    for j in range(1, GRP):
        slot = lax.rem(gi + j, GRP)
        copy(rs2.at[slot], rs2.at[slot], s_rs2.at[j], r_rs2.at[slot], partner).wait_recv()
    total = rs2[0].astype(F32)
    for j in range(1, GRP):
        total = total + rs2[j].astype(F32)

    def pick(x):
        first = jnp.sum(jnp.where(row16 == base, x, 0.0), axis=0, keepdims=True)
        second = jnp.sum(jnp.where(row16 == base + 1, x, 0.0), axis=0, keepdims=True)
        return jnp.concatenate([first, second], axis=0)

    ptk = pick(total[0:16])
    ptv = pick(total[16:32])
    unit2, inverse2 = norm(pk_ref[...].astype(F32))
    raw, _ = norm_back(ptk, unit2, inverse2, gain_k, pc16[0:2], ps16[0:2])
    pdk_ref[...] = raw.astype(BF16)
    pdv_ref[...] = ptv.astype(BF16)

    @pl.loop(1, GRP * X)
    def _(j):
        slot = lax.rem(hx * GRP + gi + j, GRP * X)
        copy(g2.at[slot], g2.at[slot], s_g2.at[j], r_g2.at[slot], partner).wait_recv()

    total = g2[0]
    for n in range(1, GRP * X):
        total = total + g2[n]
    count = (NCTX * (BLK + 2)) * X
    factor = jnp.where(row8 == 0, (count * G) ** (-0.5), count ** (-0.5))
    gg_ref[...] = (total * factor)[0:2]

    for cp in sent:
        cp.wait_send()

    @pl.when(c == 0)
    def _():
        for n in range(2):
            kv_copy(1, n, 0, 1, partner).wait_send()

    @pl.when(c == 1)
    def _():
        for n in range(2):
            kv_copy(7, n, 6, 5, partner).wait_send()

    @pl.loop(1, Z)
    def _(j):
        copy(pkv.at[z], pkv.at[z], s_ag2.at[j], r_ag2.at[z], partner).wait_send()
        copy(pterm.at[z], rs1.at[z], s_rs1.at[j], r_rs1.at[z], partner).wait_send()
        copy(g1.at[z], g1.at[z], s_g1.at[j], r_g1.at[z], partner).wait_send()

    @pl.loop(1, GRP * X)
    def _(j):
        copy(g2.at[0], g2.at[0], s_g2.at[j], r_g2.at[0], partner).wait_send()


def per_device(
    branch_q, branch_k, branch_v, branch_o, branch_dout,
    prompt_q, prompt_k, prompt_v, prompt_o, prompt_dout, gains, parents, depth,
):
    offset, level, prompt = tables()
    vmem = pl.BlockSpec(memory_space=pltpu.VMEM)
    hbm = pl.BlockSpec(memory_space=pl.ANY)
    smem = pl.BlockSpec(memory_space=pltpu.SMEM)
    dma = pltpu.SemaphoreType.DMA
    vm = pltpu.VMEM
    outs = pl.pallas_call(
        kernel,
        out_shape=(
            jax.ShapeDtypeStruct((BLK, G * HD), BF16),
            jax.ShapeDtypeStruct((BLK, HD), BF16),
            jax.ShapeDtypeStruct((BLK, HD), BF16),
            jax.ShapeDtypeStruct((2, G * HD), BF16),
            jax.ShapeDtypeStruct((2, HD), BF16),
            jax.ShapeDtypeStruct((2, HD), BF16),
            jax.ShapeDtypeStruct((2, HD), F32),
        ),
        in_specs=[vmem, hbm, hbm] + [vmem] * 8 + [smem] + [vmem] * 4,
        out_specs=(vmem,) * 7,
        scratch_shapes=[
            vm((SUB, 2, BLK, HD), BF16),
            vm((SUB, 1, HD), jnp.int32),
            vm((GRP, 32, HD), BF16),
            vm((Z, 32, HD), BF16),
            vm((ALLR, HD), BF16),
            vm((ROWS, HD), F32),
            vm((ROWS, HD), F32),
            vm((ALLR, HD), BF16),
            vm((1, ALLR), F32),
            vm((KEYS, HD), BF16),
            vm((HD, KEYS), BF16),
            vm((KEYS, HD), F32),
            vm((BLK, HD), F32),
            vm((SUB, BLK, HD), F32),
            vm((SUB, BLK, HD), F32),
            vm((SUB, 1, ROWS), jnp.int32),
            vm((KEYS, ALLR), F32),
            vm((1, ALLR), F32),
            vm((HD, ALLR), F32),
            vm((16, HD), F32),
            vm((PROWS, HD), F32),
            vm((PFX, HD), BF16),
            vm((SUB, 2, BLK, HD), BF16),
            vm((BLK, HD), F32),
            vm((BLK, HD), F32),
            vm((4, 2, BLK, HD), BF16),
            vm((3, 2, BLK, HD), BF16),
            vm((3, 2, BLK, HD), BF16),
            vm((Z, 32, HD), BF16),
            vm((Z, 32, HD), BF16),
            vm((8, HD), F32),
            vm((GRP, 32, HD), BF16),
            vm((Z, 8, HD), F32),
            vm((GRP * X, 8, HD), F32),
            dma((2,)),
            dma((8, 2)), dma((SUB, 2)),
            dma((SUB,)), dma((SUB,)),
            dma((GRP,)), dma((GRP,)),
            dma((Z,)), dma((Z,)),
            dma((4, 2)), dma((4, 2)),
            dma((3, 2)), dma((3, 2)),
            dma((Z,)), dma((Z,)),
            dma((GRP,)), dma((GRP,)),
            dma((Z,)), dma((Z,)),
            dma((GRP * X,)), dma((GRP * X,)),
        ],
        compiler_params=pltpu.CompilerParams(
            collective_id=0, has_side_effects=True, vmem_limit_bytes=60 * 1024 * 1024
        ),
        name="tree_back",
    )(
        branch_q[:, 0], branch_k[:, 0], branch_v[:, 0], branch_o[:, 0], branch_dout[:, 0],
        prompt_q[:, 0], prompt_k[:, 0], prompt_v[:, 0], prompt_o[:, 0], prompt_dout[:, 0],
        gains, parents, depth.reshape(1, BLK),
        jnp.asarray(offset), jnp.asarray(level), jnp.asarray(prompt),
    )
    dq, dk, dv, pdq, pdk, pdv, gain_grads = outs
    return (
        dq[:, None], dk[:, None], dv[:, None], pdq[:, None], pdk[:, None], pdv[:, None], gain_grads,
    )


def solution(mesh):
    tok = P("ctx", "head", None)
    return jax.shard_map(
        per_device,
        mesh=mesh,
        in_specs=(tok,) * 10 + (P(), P("ctx"), P("ctx")),
        out_specs=(tok,) * 6 + (P(),),
        check_vma=False,
    )
```

```python
import math

import numpy as np

import jax
import jax.numpy as jnp
from jax import lax
from jax.experimental import pallas as pl
from jax.experimental.pallas import tpu as pltpu
from jax.sharding import PartitionSpec as P

HD = 128
G = 8
BLK = 128
SUB = 8
PFX = 256
EPS = 1e-06
THETA = 1000000.0
Y = 4
Z = 16
GRP = 2 * Y
X = 4
JUMP = 4
NCTX = Y * Z * 2
ROWS = BLK * G
PROWS = 128
ALLR = ROWS + PROWS
KEYS = PFX + SUB * BLK
SCALE = HD ** (-0.5)
EXP2_SCALE = SCALE * math.log2(math.e)
MESH = pl.DeviceIdType.MESH
F32 = jnp.float32
BF16 = jnp.bfloat16


def prompt_order():
    p = np.arange(PFX)
    return (p // 64) * 64 + (p // 2 % Z) * 4 + (p // 32 % 2) * 2 + p % 2


def tables():
    freq = THETA ** (-(np.arange(HD // 2, dtype=np.float64) * 2.0) / HD)

    def pair(positions):
        angle = positions[:, None].astype(np.float64) * freq[None, :]
        cosine, sine = np.cos(angle), np.sin(angle)
        return np.stack(
            [np.concatenate([cosine, cosine], 1), np.concatenate([-sine, sine], 1)]
        ).astype(np.float32)

    offset = pair(np.arange(BLK))
    level = pair(np.arange(16) * BLK)
    prompt = pair(prompt_order())
    return offset, level, prompt


def norm(x):
    inverse = lax.rsqrt(jnp.mean(x * x, axis=-1, keepdims=True) + EPS)
    return x * inverse, inverse


def swap(x):
    return pltpu.roll(x, HD // 2, 1)


def rotate(x, c, s):
    return x * c + swap(x) * s


def unrotate(x, c, s):
    return x * c - swap(x) * s


def norm_back(grad, unit, inverse, gain, c, s):
    g = unrotate(grad, c, s)
    u = g * gain
    raw = (u - unit * jnp.mean(u * unit, axis=-1, keepdims=True)) * inverse
    return raw, jnp.sum(g * unit, axis=0, keepdims=True)


def nt(a, b):
    return lax.dot_general(a, b, (((1,), (1,)), ((), ())), preferred_element_type=F32)


def nn(a, b):
    return lax.dot_general(a, b, (((1,), (0,)), ((), ())), preferred_element_type=F32)


def kernel(
    q_hbm, k_hbm, v_hbm, o_hbm, do_hbm, pq_ref, pk_ref, pv_ref, po_ref, pdo_ref,
    gains_ref, par_ref, depth_ref, toff_hbm, tlev_ref, tpr_hbm,
    dq_ref, dk_ref, dv_ref, pdq_ref, pdk_ref, pdv_ref, gg_ref,
    q_ref, o_ref, do_ref, toff_ref, tpr_ref,
    kv, parw, zr, grp,
    qrot, qunit, qinv, dor, delta, krot, krott, kunit, kinv, ctab, stab, thr, eh, dsb, tot, dqt,
    qs, dos, scr, pscr, dn, vp,
    wterm, ownk, ownv, prx, mtx, mrx, pterm, rs1, rs2t, rs2, g1, g2,
    s_loc, s_kv, r_kv, s_par, r_par, s_zr, r_zr, s_ag2, r_ag2,
    s_p, r_p, s_m, r_m, s_rs1, r_rs1, s_rs2, r_rs2, s_g1, r_g1, s_g2, r_g2,
):
    me = lax.axis_index("ctx")
    hx = lax.axis_index("head")
    y = me // (2 * Z)
    z = lax.rem(me // 2, Z)
    c = lax.rem(me, 2)
    gi = y * 2 + c
    partner = me + 1 - 2 * c

    def at(offset):
        return lax.rem(me + (offset + NCTX), NCTX)

    def grp_dev(index):
        return ((index // 2) * Z + z) * 2 + lax.rem(index, 2)

    def z_dev(index):
        return (y * Z + index) * 2 + c

    def z_at(offset):
        return lax.rem(z + (offset + Z), Z)

    def copy(src, dst, ssem, rsem, device, head=None):
        where = {"ctx": device} if head is None else {"ctx": device, "head": head}
        return pltpu.make_async_remote_copy(
            src_ref=src, dst_ref=dst, send_sem=ssem, recv_sem=rsem,
            device_id=where, device_id_type=MESH,
        )

    barrier = pltpu.get_barrier_semaphore()

    def greet(device, head=None):
        where = {"ctx": device} if head is None else {"ctx": device, "head": head}
        pl.semaphore_signal(barrier, inc=1, device_id=where, device_id_type=MESH)

    for offset in (-7, -6, -5, -4, -3, -2, -1, 1, 2):
        greet(at(offset))
    for offset in range(1, JUMP + 1):
        greet(z_dev(z_at(offset)))
        greet(z_dev(z_at(-offset)))

    @pl.loop(1, GRP * X)
    def _(j):
        other = lax.rem(hx * GRP + gi + j, GRP * X)
        greet(grp_dev(lax.rem(other, GRP)), other // GRP)

    own = [
        pltpu.make_async_copy(k_hbm, kv.at[0, 0], s_loc.at[0]),
        pltpu.make_async_copy(v_hbm, kv.at[0, 1], s_loc.at[1]),
    ]
    later = [
        pltpu.make_async_copy(src, dst, s_loc.at[n])
        for n, src, dst in (
            (2, toff_hbm, toff_ref), (3, q_hbm, q_ref), (4, do_hbm, do_ref),
            (5, o_hbm, o_ref), (6, tpr_hbm, tpr_ref),
        )
    ]
    for cp in own + later:
        cp.start()
    parw[0] = jnp.full((1, HD), par_ref[0], jnp.int32)
    zr[z, 0] = pk_ref[...]
    zr[z, 1] = pv_ref[...]
    for cp in own:
        cp.wait()
    pl.semaphore_wait(barrier, 9 + 2 * JUMP + (GRP * X - 1))

    def kv_copy(op, n, src, dst, device):
        return copy(kv.at[src, n], kv.at[dst, n], s_kv.at[op, n], r_kv.at[dst, n], device)

    def kv_arrived(slot):
        for n in range(2):
            copy(kv.at[slot, n], kv.at[slot, n], s_kv.at[0, n], r_kv.at[slot, n], partner).wait_recv()

    sent = []

    def send(cp):
        cp.start()
        sent.append(cp)

    def zr_send(op, slot, to):
        send(copy(zr.at[slot], zr.at[slot], s_zr.at[op], r_zr.at[slot], z_dev(to)))

    def zr_arrived(slot):
        copy(zr.at[slot], zr.at[slot], s_zr.at[0], r_zr.at[slot], partner).wait_recv()

    for j in range(JUMP, 0, -1):
        zr_send(j, z, z_at(j))
        zr_send(JUMP + j, z, z_at(-j))
    for d in range(1, SUB):
        send(copy(parw.at[0], parw.at[d], s_par.at[d], r_par.at[d], at(d)))
    for n in range(2):
        send(kv_copy(0, n, 0, 2, at(2)))

    @pl.when(c == 0)
    def _():
        for n in range(2):
            kv_copy(1, n, 0, 1, partner).start()

    row16 = lax.broadcasted_iota(jnp.int32, (16, HD), 0)
    gain_q = gains_ref[0:1, :]
    gain_k = gains_ref[1:2, :]
    lane1 = lax.broadcasted_iota(jnp.int32, (1, HD), 1)
    level = (depth_ref[...] - lane1) >> 7

    def level_rows(lv):
        cl = jnp.zeros((1, HD), F32)
        sl = jnp.zeros((1, HD), F32)
        for n in range(1, SUB + 2):
            cl = jnp.where(lv == n, tlev_ref[0, n : n + 1, :], cl)
            sl = jnp.where(lv == n, tlev_ref[1, n : n + 1, :], sl)
        return cl, sl

    def block_tables(d, lv):
        cl, sl = level_rows(lv)
        co, so = toff_ref[0], toff_ref[1]
        ctab[d] = co * cl - so * sl
        stab[d] = so * cl + co * sl

    for cp in later:
        cp.wait()
    block_tables(0, level)

    @pl.loop(0, G)
    def _(g):
        lanes = pl.ds(pl.multiple_of(g * HD, HD), HD)
        rows = pl.ds(pl.multiple_of(g * BLK, BLK), BLK)
        unit, inverse = norm(q_ref[:, lanes].astype(F32))
        qunit[rows, :] = unit
        qinv[rows, :] = jnp.broadcast_to(inverse, (BLK, HD))
        qrot[rows, :] = rotate(unit * gain_q, ctab[0], stab[0]).astype(BF16)
        d = do_ref[:, lanes]
        dor[rows, :] = d
        prod = d.astype(F32) * o_ref[:, lanes].astype(F32)
        delta[:, lanes] = jnp.sum(prod.T, axis=0, keepdims=True)

    kv_arrived(2)
    for n in range(2):
        send(kv_copy(2, n, 2, 4, at(2)))
        send(kv_copy(3, n, 2, 3 - 2 * c, partner))
    for j in range(1, JUMP + 1):
        zr_arrived(z_at(-j))
        zr_send(2 * JUMP + j, z_at(-j), z_at(JUMP))
        zr_arrived(z_at(j))
        if j < JUMP:
            zr_send(3 * JUMP + j, z_at(j), z_at(-JUMP))

    def to_rows(ref):
        x = ref[...].astype(F32)
        for g in range(G):
            scr[2 * g : 2 * g + 2, :] = x[:, g * HD : (g + 1) * HD]
        return scr[0:16, :]

    pslot = gi * 32 + z * 2
    odd = lax.rem(row16, 2) == 1

    def prow(n):
        first = jnp.broadcast_to(tpr_ref[n, pl.ds(pslot, 1), :], (16, HD))
        second = jnp.broadcast_to(tpr_ref[n, pl.ds(pslot + 1, 1), :], (16, HD))
        return jnp.where(odd, second, first)

    pc16, ps16 = prow(0), prow(1)
    prest = pl.ds(ROWS + 16, PROWS - 16)
    punit, pinverse = norm(to_rows(pq_ref))
    qrot[ROWS : ROWS + 16, :] = rotate(punit * gain_q, pc16, ps16).astype(BF16)
    qrot[prest, :] = jnp.zeros((PROWS - 16, HD), BF16)
    pd = to_rows(pdo_ref)
    dor[ROWS : ROWS + 16, :] = pd.astype(BF16)
    dor[prest, :] = jnp.zeros((PROWS - 16, HD), BF16)
    pscr[...] = jnp.zeros((PROWS, HD), F32)
    pscr[0:16, :] = pd * to_rows(po_ref)
    delta[:, ROWS:] = jnp.sum(pscr[...].T, axis=0, keepdims=True)

    tot[...] = jnp.zeros((1, ALLR), F32)
    dqt[...] = jnp.zeros((HD, ALLR), F32)

    def attend(krows, vals, width, visible):
        s = nt(krot[krows, :], qrot[0:width, :])
        e = jnp.where(visible, jnp.exp2(s * EXP2_SCALE), 0.0)
        tot[:, 0:width] += jnp.sum(e, axis=0, keepdims=True)
        eh[krows, 0:width] = e.astype(BF16)
        dp = nt(vals, dor[0:width, :])
        ds = (e * (dp - delta[:, 0:width])).astype(BF16)
        dsb[krows, 0:width] = ds
        dqt[:, 0:width] += nn(krott[:, krows], ds)

    def key_block(d):
        rows = slice(PFX + d * BLK, PFX + (d + 1) * BLK)
        unit, inverse = norm(kv[d, 0].astype(F32))
        if d == 0:
            kinv[...] = jnp.broadcast_to(inverse, (BLK, HD))
        kunit[rows, :] = unit
        rot = rotate(unit * gain_k, ctab[d], stab[d])
        krot[rows, :] = rot.astype(BF16)
        krott[:, rows] = rot.T.astype(BF16)

    def wide(x):
        return jnp.concatenate([x] * G, axis=1)

    def window(first, count):
        for d in range(first, first + count):
            key_block(d)
        offs = lax.broadcasted_iota(jnp.int32, (BLK, ROWS), 0)
        visible = jnp.concatenate([offs <= thr[d] for d in range(first, first + count)], axis=0)
        vals = kv[first : first + count, 1].reshape(count * BLK, HD)
        attend(slice(PFX + first * BLK, PFX + (first + count) * BLK), vals, ROWS, visible)

    thr[0] = wide(lane1)
    window(0, 1)

    kv_arrived(4)
    for n in range(2):
        send(kv_copy(4, n, 4, 6, at(2)))
        send(kv_copy(5, n, 4, 5 - 2 * c, partner))

    for d in range(1, SUB):
        copy(parw.at[d], parw.at[d], s_par.at[d], r_par.at[d], partner).wait_recv()
    block = me + PFX // BLK
    current = jnp.full((1, HD), block, jnp.int32)
    seen = [jnp.zeros((1, HD), jnp.int32) for _ in range(SUB)]
    levels = [jnp.zeros((1, HD), jnp.int32) for _ in range(SUB)]
    above = [parw[d] for d in range(SUB)]
    for step in range(SUB + 1):
        branchy = current >= PFX // BLK
        upward = jnp.zeros((1, HD), jnp.int32)
        for d in range(SUB):
            match = (current == block - d) & branchy
            seen[d] = jnp.where(match, 1, seen[d])
            levels[d] = jnp.where(match, level - step, levels[d])
            upward = jnp.where(match, above[d], upward)
        current = jnp.where(branchy, upward, current)
    fork = current
    for d in range(1, SUB):
        thr[d] = jnp.where(wide(seen[d]) == 1, BLK, -1)
        block_tables(d, levels[d])
    thr_prompt = jnp.concatenate(
        [wide(BLK * (fork + 1) - 1), me * 2 + lax.rem(lane1, 2)], axis=1
    )

    kv_arrived(1)
    window(1, 2)

    kv_arrived(6)
    for n in range(2):
        send(kv_copy(6, n, 6, 7, at(1)))

    @pl.when(c == 1)
    def _():
        for n in range(2):
            kv_copy(7, n, 6, 5, partner).start()

    for j in range(JUMP + 1, 2 * JUMP + 1):
        zr_arrived(z_at(-j))
        if j < 2 * JUMP:
            zr_arrived(z_at(j))
    for n in range(2):
        for k in range(Z):
            dn[n * 32 + 2 * k : n * 32 + 2 * k + 2, :] = zr[k, n].astype(F32)
    grp[gi] = dn[...].astype(BF16)
    kv_arrived(3)
    for j in range(1, GRP):
        send(copy(grp.at[gi], grp.at[gi], s_ag2.at[j], r_ag2.at[gi], grp_dev(lax.rem(gi + j, GRP))))
    window(3, 2)
    kv_arrived(5)
    kv_arrived(7)
    window(5, 3)

    for j in range(1, GRP):
        slot = lax.rem(gi + j, GRP)
        copy(grp.at[slot], grp.at[slot], s_ag2.at[j], r_ag2.at[slot], partner).wait_recv()
    pcos, psin = tpr_ref[0], tpr_ref[1]
    pk_all = jnp.concatenate([grp[n, 0:32, :] for n in range(GRP)], axis=0).astype(F32)
    pv_all = jnp.concatenate([grp[n, 32:64, :] for n in range(GRP)], axis=0)
    pkunit, _ = norm(pk_all)
    rot = rotate(pkunit * gain_k, pcos, psin)
    krot[0:PFX, :] = rot.astype(BF16)
    krott[:, 0:PFX] = rot.T.astype(BF16)
    kunit[0:PFX, :] = pkunit
    p_key = lax.broadcasted_iota(jnp.int32, (PFX, ALLR), 0)
    t_key = ((p_key >> 6) << 6) + (((p_key >> 1) & 15) << 2) + (((p_key >> 5) & 1) << 1) + (p_key & 1)
    attend(slice(0, PFX), pv_all, ALLR, t_key <= thr_prompt)

    tot[...] = 1.0 / tot[...]
    for g in range(G + 1):
        rows = slice(g * BLK, (g + 1) * BLK)
        column = jnp.broadcast_to(tot[:, rows], (BLK, BLK)).T
        qs[rows, :] = (qrot[rows, :].astype(F32) * column).astype(BF16)
        dos[rows, :] = (dor[rows, :].astype(F32) * column).astype(BF16)

    def key_grads(krows, width):
        dk = nn(dsb[krows, 0:width], qs[0:width, :]) * SCALE
        return dk, nn(eh[krows, 0:width], dos[0:width, :])

    dk, dv = key_grads(slice(0, PFX), ALLR)
    for n in range(GRP):
        pterm[n, 0:32, :] = dk[n * 32 : (n + 1) * 32].astype(BF16)
        pterm[n, 32:64, :] = dv[n * 32 : (n + 1) * 32].astype(BF16)
    gk = jnp.sum(unrotate(dk, pcos, psin) * kunit[0:PFX, :], axis=0, keepdims=True)
    for j in range(1, GRP):
        other = lax.rem(gi + j, GRP)
        send(copy(pterm.at[other], rs1.at[gi], s_rs1.at[j], r_rs1.at[gi], grp_dev(other)))

    dk, dv = key_grads(slice(PFX, KEYS), ROWS)
    for d in range(SUB - 1, -1, -1):
        rows = slice(d * BLK, (d + 1) * BLK)
        if d:
            wterm[d, 0] = dk[rows].astype(BF16)
            wterm[d, 1] = dv[rows].astype(BF16)
        else:
            ownk[...] = dk[rows]
            ownv[...] = dv[rows]
        g_part = unrotate(dk[rows], ctab[d], stab[d]) * kunit[PFX + d * BLK : PFX + (d + 1) * BLK, :]
        gk = gk + jnp.sum(g_part, axis=0, keepdims=True)
    for n in range(2):
        send(copy(wterm.at[7, n], prx.at[3, n], s_p.at[3, n], r_p.at[3, n], at(-1)))
    for slot in (2, 1, 0):
        for n in range(2):
            send(copy(wterm.at[2 * slot + 1, n], prx.at[slot, n], s_p.at[slot, n], r_p.at[slot, n], partner))

    gq = jnp.zeros((1, HD), F32)
    for g in range(G):
        rows = slice(g * BLK, (g + 1) * BLK)
        grad = (dqt[:, rows] * (tot[:, rows] * SCALE)).T
        raw, part = norm_back(grad, qunit[rows, :], qinv[rows, :], gain_q, ctab[0], stab[0])
        dq_ref[:, rows] = raw.astype(BF16)
        gq = gq + part
    grad = (dqt[:, ROWS:] * (tot[:, ROWS:] * SCALE)).T[0:16]
    raw, part = norm_back(grad, punit, pinverse, gain_q, pc16, ps16)
    gq = gq + part
    row8 = lax.broadcasted_iota(jnp.int32, (8, HD), 0)
    g1[z] = jnp.where(row8 == 0, gq, jnp.where(row8 == 1, gk, 0.0))
    scr[...] = raw
    for g in range(G):
        pdq_ref[:, g * HD : (g + 1) * HD] = scr[2 * g : 2 * g + 2, :].astype(BF16)

    @pl.loop(1, Z)
    def _(j):
        copy(g1.at[z], g1.at[z], s_g1.at[j], r_g1.at[z], z_dev(lax.rem(z + j, Z))).start()

    def p_arrived(slot, n):
        copy(prx.at[slot, n], prx.at[slot, n], s_p.at[slot, n], r_p.at[slot, n], partner).wait_recv()

    def m_arrived(k, n):
        copy(mrx.at[k, n], mrx.at[k, n], s_m.at[k, n], r_m.at[k, n], partner).wait_recv()

    def step_down(k):
        for n in range(2):
            if k < 3:
                m_arrived(k, n)
            value = wterm[2 * k, n].astype(F32) + prx[k - c, n].astype(F32)
            if k == 3:
                value = value + jnp.where(c == 1, prx[3, n].astype(F32), 0.0)
            else:
                value = value + mrx[k, n].astype(F32)
            mtx[k - 1, n] = value.astype(BF16)
        for n in range(2):
            send(copy(mtx.at[k - 1, n], mrx.at[k - 1, n], s_m.at[k - 1, n], r_m.at[k - 1, n], at(-2)))

    for slot in range(4):
        for n in range(2):
            p_arrived(slot, n)
    step_down(3)

    for j in range(1, GRP):
        slot = lax.rem(gi + j, GRP)
        copy(rs1.at[slot], rs1.at[slot], s_rs1.at[j], r_rs1.at[slot], partner).wait_recv()
    rs1[gi] = pterm[gi]
    total = rs1[0].astype(F32)
    for n in range(1, GRP):
        total = total + rs1[n].astype(F32)
    dn[...] = total
    for n in range(2):
        for k in range(Z):
            rs2t[k, n] = dn[n * 32 + 2 * k : n * 32 + 2 * k + 2, :]
    rs2[z] = rs2t[z]

    @pl.loop(1, Z)
    def _(j):
        other = lax.rem(z + j, Z)
        copy(rs2t.at[other], rs2.at[z], s_rs2.at[j], r_rs2.at[z], z_dev(other)).start()

    step_down(2)

    @pl.loop(1, Z)
    def _(j):
        slot = lax.rem(z + j, Z)
        copy(g1.at[slot], g1.at[slot], s_g1.at[j], r_g1.at[slot], partner).wait_recv()

    total = g1[0]
    for n in range(1, Z):
        total = total + g1[n]
    xg = hx * GRP + gi
    g2[xg] = total

    @pl.loop(1, GRP * X)
    def _(j):
        other = lax.rem(xg + j, GRP * X)
        copy(
            g2.at[xg], g2.at[xg], s_g2.at[j], r_g2.at[xg], grp_dev(lax.rem(other, GRP)), other // GRP
        ).start()

    step_down(1)

    for n, total_ref in ((0, ownk), (1, ownv)):
        m_arrived(0, n)
        total_ref[...] += mrx[0, n].astype(F32)

        @pl.when(c == 0)
        def _():
            total_ref[...] += prx[0, n].astype(F32)

    raw, _ = norm_back(
        ownk[...], kunit[PFX : PFX + BLK, :], kinv[...], gain_k, ctab[0], stab[0]
    )
    dk_ref[...] = raw.astype(BF16)
    dv_ref[...] = ownv[...].astype(BF16)

    @pl.loop(1, Z)
    def _(j):
        slot = lax.rem(z + j, Z)
        copy(rs2.at[slot], rs2.at[slot], s_rs2.at[j], r_rs2.at[slot], partner).wait_recv()

    ptk, ptv = rs2[0, 0], rs2[0, 1]
    for n in range(1, Z):
        ptk = ptk + rs2[n, 0]
        ptv = ptv + rs2[n, 1]
    unit2, inverse2 = norm(pk_ref[...].astype(F32))
    raw, _ = norm_back(ptk, unit2, inverse2, gain_k, pc16[0:2], ps16[0:2])
    pdk_ref[...] = raw.astype(BF16)
    pdv_ref[...] = ptv.astype(BF16)

    @pl.loop(1, GRP * X)
    def _(j):
        slot = lax.rem(xg + j, GRP * X)
        copy(g2.at[slot], g2.at[slot], s_g2.at[j], r_g2.at[slot], partner).wait_recv()

    total = g2[0]
    for n in range(1, GRP * X):
        total = total + g2[n]
    count = (NCTX * (BLK + 2)) * X
    factor = jnp.where(row8 == 0, (count * G) ** (-0.5), count ** (-0.5))
    gg_ref[...] = (total * factor)[0:2]

    for cp in sent:
        cp.wait_send()

    @pl.when(c == 0)
    def _():
        for n in range(2):
            kv_copy(1, n, 0, 1, partner).wait_send()

    @pl.when(c == 1)
    def _():
        for n in range(2):
            kv_copy(7, n, 6, 5, partner).wait_send()

    @pl.loop(1, Z)
    def _(j):
        copy(rs2t.at[z], rs2.at[z], s_rs2.at[j], r_rs2.at[z], partner).wait_send()
        copy(g1.at[z], g1.at[z], s_g1.at[j], r_g1.at[z], partner).wait_send()

    @pl.loop(1, GRP * X)
    def _(j):
        copy(g2.at[0], g2.at[0], s_g2.at[j], r_g2.at[0], partner).wait_send()


def per_device(
    branch_q, branch_k, branch_v, branch_o, branch_dout,
    prompt_q, prompt_k, prompt_v, prompt_o, prompt_dout, gains, parents, depth,
):
    offset, level, prompt = tables()
    vmem = pl.BlockSpec(memory_space=pltpu.VMEM)
    hbm = pl.BlockSpec(memory_space=pl.ANY)
    smem = pl.BlockSpec(memory_space=pltpu.SMEM)
    dma = pltpu.SemaphoreType.DMA
    vm = pltpu.VMEM
    outs = pl.pallas_call(
        kernel,
        out_shape=(
            jax.ShapeDtypeStruct((BLK, G * HD), BF16),
            jax.ShapeDtypeStruct((BLK, HD), BF16),
            jax.ShapeDtypeStruct((BLK, HD), BF16),
            jax.ShapeDtypeStruct((2, G * HD), BF16),
            jax.ShapeDtypeStruct((2, HD), BF16),
            jax.ShapeDtypeStruct((2, HD), BF16),
            jax.ShapeDtypeStruct((2, HD), F32),
        ),
        in_specs=[hbm] * 5 + [vmem] * 6 + [smem, vmem, hbm, vmem, hbm],
        out_specs=(vmem,) * 7,
        scratch_shapes=[
            vm((BLK, G * HD), BF16),
            vm((BLK, G * HD), BF16),
            vm((BLK, G * HD), BF16),
            vm((2, BLK, HD), F32),
            vm((2, PFX, HD), F32),
            vm((SUB, 2, BLK, HD), BF16),
            vm((SUB, 1, HD), jnp.int32),
            vm((Z, 2, 2, HD), BF16),
            vm((GRP, 64, HD), BF16),
            vm((ALLR, HD), BF16),
            vm((ROWS, HD), F32),
            vm((ROWS, HD), F32),
            vm((ALLR, HD), BF16),
            vm((1, ALLR), F32),
            vm((KEYS, HD), BF16),
            vm((HD, KEYS), BF16),
            vm((KEYS, HD), F32),
            vm((BLK, HD), F32),
            vm((SUB, BLK, HD), F32),
            vm((SUB, BLK, HD), F32),
            vm((SUB, 1, ROWS), jnp.int32),
            vm((KEYS, ALLR), BF16),
            vm((KEYS, ALLR), BF16),
            vm((1, ALLR), F32),
            vm((HD, ALLR), F32),
            vm((ALLR, HD), BF16),
            vm((ALLR, HD), BF16),
            vm((16, HD), F32),
            vm((PROWS, HD), F32),
            vm((64, HD), F32),
            vm((PFX, HD), BF16),
            vm((SUB, 2, BLK, HD), BF16),
            vm((BLK, HD), F32),
            vm((BLK, HD), F32),
            vm((4, 2, BLK, HD), BF16),
            vm((3, 2, BLK, HD), BF16),
            vm((3, 2, BLK, HD), BF16),
            vm((GRP, 64, HD), BF16),
            vm((GRP, 64, HD), BF16),
            vm((Z, 2, 2, HD), F32),
            vm((Z, 2, 2, HD), F32),
            vm((Z, 8, HD), F32),
            vm((GRP * X, 8, HD), F32),
            dma((7,)),
            dma((8, 2)), dma((SUB, 2)),
            dma((SUB,)), dma((SUB,)),
            dma((4 * JUMP + 1,)), dma((Z,)),
            dma((GRP,)), dma((GRP,)),
            dma((4, 2)), dma((4, 2)),
            dma((3, 2)), dma((3, 2)),
            dma((GRP,)), dma((GRP,)),
            dma((Z,)), dma((Z,)),
            dma((Z,)), dma((Z,)),
            dma((GRP * X,)), dma((GRP * X,)),
        ],
        compiler_params=pltpu.CompilerParams(
            collective_id=0, has_side_effects=True, vmem_limit_bytes=60 * 1024 * 1024
        ),
        name="tree_back",
    )(
        branch_q[:, 0], branch_k[:, 0], branch_v[:, 0], branch_o[:, 0], branch_dout[:, 0],
        prompt_q[:, 0], prompt_k[:, 0], prompt_v[:, 0], prompt_o[:, 0], prompt_dout[:, 0],
        gains, parents, depth.reshape(1, BLK),
        jnp.asarray(offset), jnp.asarray(level), jnp.asarray(prompt),
    )
    dq, dk, dv, pdq, pdk, pdv, gain_grads = outs
    return (
        dq[:, None], dk[:, None], dv[:, None], pdq[:, None], pdk[:, None], pdv[:, None], gain_grads,
    )


def solution(mesh):
    tok = P("ctx", "head", None)
    return jax.shard_map(
        per_device,
        mesh=mesh,
        in_specs=(tok,) * 10 + (P(), P("ctx"), P("ctx")),
        out_specs=(tok,) * 6 + (P(),),
        check_vma=False,
    )
```

```python
import math

import numpy as np

import jax
import jax.numpy as jnp
from jax import lax
from jax.experimental import pallas as pl
from jax.experimental.pallas import tpu as pltpu
from jax.sharding import PartitionSpec as P

HD = 128
G = 8
BLK = 128
SUB = 8
PFX = 256
EPS = 1e-06
THETA = 1000000.0
Y = 4
Z = 16
GRP = 2 * Y
X = 4
JUMP = 4
NCTX = Y * Z * 2
ROWS = BLK * G
PROWS = 128
ALLR = ROWS + PROWS
KEYS = PFX + SUB * BLK
SCALE = HD ** (-0.5)
EXP2_SCALE = SCALE * math.log2(math.e)
MESH = pl.DeviceIdType.MESH
F32 = jnp.float32
BF16 = jnp.bfloat16


def prompt_order():
    p = np.arange(PFX)
    return (p // 64) * 64 + (p // 2 % Z) * 4 + (p // 32 % 2) * 2 + p % 2


def tables():
    freq = THETA ** (-(np.arange(HD // 2, dtype=np.float64) * 2.0) / HD)

    def pair(positions):
        angle = positions[:, None].astype(np.float64) * freq[None, :]
        cosine, sine = np.cos(angle), np.sin(angle)
        return np.stack(
            [np.concatenate([cosine, cosine], 1), np.concatenate([-sine, sine], 1)]
        ).astype(np.float32)

    offset = pair(np.arange(BLK))
    level = pair(np.arange(16) * BLK)
    prompt = pair(prompt_order())
    return offset, level, prompt


def norm(x):
    inverse = lax.rsqrt(jnp.mean(x * x, axis=-1, keepdims=True) + EPS)
    return x * inverse, inverse


def swap(x):
    return pltpu.roll(x, HD // 2, 1)


def rotate(x, c, s):
    return x * c + swap(x) * s


def unrotate(x, c, s):
    return x * c - swap(x) * s


def norm_back(grad, unit, inverse, gain, c, s):
    g = unrotate(grad, c, s)
    u = g * gain
    raw = (u - unit * jnp.mean(u * unit, axis=-1, keepdims=True)) * inverse
    return raw, jnp.sum(g * unit, axis=0, keepdims=True)


def nt(a, b):
    return lax.dot_general(a, b, (((1,), (1,)), ((), ())), preferred_element_type=F32)


def nn(a, b):
    return lax.dot_general(a, b, (((1,), (0,)), ((), ())), preferred_element_type=F32)


def kernel(
    q_hbm, k_hbm, v_hbm, o_hbm, do_hbm, pq_hbm, pk_hbm, pv_hbm, po_hbm, pdo_hbm,
    gains_hbm, par_hbm, depth_hbm, tab_hbm,
    dq_hbm, dk_ref, dv_ref, pdq_ref, pdk_ref, pdv_ref, gg_ref,
    qod, pqod, tab, dq_ref, gains_ref, par_ref, depth_ref,
    kv, parw, zr, grp,
    qrot, qunit, qinv, dor, delta, krot, krott, kunit, kinv, ctab, stab, thr, eh, dsb, tot, dqt,
    qs, dos, scr, pscr, dn,
    wterm, ownk, ownv, prx, mtx, mrx, pterm, rs1, rs2t, rs2, g1, g2,
    s_loc, s_kv, r_kv, s_par, r_par, s_zr, r_zr, s_ag2, r_ag2,
    s_p, r_p, s_m, r_m, s_rs1, r_rs1, s_rs2, r_rs2, s_g1, r_g1, s_g2, r_g2,
):
    me = lax.axis_index("ctx")
    hx = lax.axis_index("head")
    y = me // (2 * Z)
    z = lax.rem(me // 2, Z)
    c = lax.rem(me, 2)
    gi = y * 2 + c
    partner = me + 1 - 2 * c

    def at(offset):
        return lax.rem(me + (offset + NCTX), NCTX)

    def grp_dev(index):
        return ((index // 2) * Z + z) * 2 + lax.rem(index, 2)

    def z_dev(index):
        return (y * Z + index) * 2 + c

    def z_at(offset):
        return lax.rem(z + (offset + Z), Z)

    def copy(src, dst, ssem, rsem, device, head=None):
        where = {"ctx": device} if head is None else {"ctx": device, "head": head}
        return pltpu.make_async_remote_copy(
            src_ref=src, dst_ref=dst, send_sem=ssem, recv_sem=rsem,
            device_id=where, device_id_type=MESH,
        )

    barrier = pltpu.get_barrier_semaphore()

    def greet(device, head=None):
        where = {"ctx": device} if head is None else {"ctx": device, "head": head}
        pl.semaphore_signal(barrier, inc=1, device_id=where, device_id_type=MESH)

    for offset in (-7, -6, -5, -4, -3, -2, -1, 1, 2):
        greet(at(offset))
    for offset in range(1, JUMP + 1):
        greet(z_dev(z_at(offset)))
        greet(z_dev(z_at(-offset)))

    @pl.loop(1, GRP * X)
    def _(j):
        other = lax.rem(hx * GRP + gi + j, GRP * X)
        greet(grp_dev(lax.rem(other, GRP)), other // GRP)

    def fetch(n, src, dst):
        cp = pltpu.make_async_copy(src, dst, s_loc.at[n])
        cp.start()
        return cp

    par_in = fetch(0, par_hbm, par_ref)
    fetch(1, pk_hbm, zr.at[z, 0])
    fetch(1, pv_hbm, zr.at[z, 1])
    fetch(2, k_hbm, kv.at[0, 0])
    fetch(2, v_hbm, kv.at[0, 1])
    later = [fetch(3, gains_hbm, gains_ref), fetch(4, depth_hbm, depth_ref), fetch(5, tab_hbm, tab)]
    for n, (big, small) in enumerate(((q_hbm, pq_hbm), (o_hbm, po_hbm), (do_hbm, pdo_hbm))):
        fetch(6, big, qod.at[n])
        fetch(7, small, pqod.at[n])
    toff_ref = tab.at[:, 0:BLK]
    tlev_ref = tab.at[:, BLK : BLK + 16]
    tpr_ref = tab.at[:, BLK + 16 :]

    def fetched(n, ref):
        pltpu.make_async_copy(ref, ref, s_loc.at[n]).wait()

    par_in.wait()
    fetched(1, zr.at[z])
    fetched(2, kv.at[0])
    parw[0] = jnp.broadcast_to(par_ref[...], (1, HD))
    pl.semaphore_wait(barrier, 9 + 2 * JUMP + (GRP * X - 1))

    def kv_copy(n, src, dst, device):
        return copy(kv.at[src, n], kv.at[dst, n], s_kv.at[0], r_kv.at[dst, n], device)

    def kv_arrived(slot, halves=(0, 1)):
        for n in halves:
            copy(kv.at[slot, n], kv.at[slot, n], s_kv.at[0], r_kv.at[slot, n], partner).wait_recv()

    def send(cp):
        cp.start()

    def sum_wait(ref, count, sem):
        part = ref.at[pl.ds(0, count)]
        copy(part, part, sem, sem, partner).wait_recv()

    def sent(ref, count, sem):
        part = ref.at[pl.ds(0, count)]
        copy(part, part, sem, sem, partner).wait_send()

    def zr_send(far, slot, to):
        copy(zr.at[slot], zr.at[slot], s_zr.at[0], r_zr.at[far], z_dev(to)).start()

    for j in range(JUMP, 0, -1):
        zr_send(0, z, z_at(j))
        zr_send(0, z, z_at(-j))
    for d in range(1, SUB):
        send(copy(parw.at[0], parw.at[d], s_par.at[0], r_par.at[0], at(d)))
    for n in range(2):
        send(kv_copy(n, 0, 2, at(2)))

    @pl.when(c == 0)
    def _():
        for n in range(2):
            kv_copy(n, 0, 1, partner).start()

    row16 = lax.broadcasted_iota(jnp.int32, (16, HD), 0)
    for cp in later:
        cp.wait()
    fetched(6, qod)
    fetched(7, pqod)
    gain_q = gains_ref[0:1, :]
    gain_k = gains_ref[1:2, :]
    lane1 = lax.broadcasted_iota(jnp.int32, (1, HD), 1)
    level = (depth_ref[...] - lane1) >> 7

    def level_rows(lv):
        cl = jnp.zeros((1, HD), F32)
        sl = jnp.zeros((1, HD), F32)
        for n in range(1, SUB + 2):
            cl = jnp.where(lv == n, tlev_ref[0, n : n + 1, :], cl)
            sl = jnp.where(lv == n, tlev_ref[1, n : n + 1, :], sl)
        return cl, sl

    def block_tables(d, lv):
        cl, sl = level_rows(lv)
        co, so = toff_ref[0], toff_ref[1]
        ctab[d] = co * cl - so * sl
        stab[d] = so * cl + co * sl

    block_tables(0, level)

    @pl.loop(0, G)
    def _(g):
        lanes = pl.ds(pl.multiple_of(g * HD, HD), HD)
        rows = pl.ds(pl.multiple_of(g * BLK, BLK), BLK)
        unit, inverse = norm(qod[0, :, lanes].astype(F32))
        qunit[rows, :] = unit
        qinv[rows, :] = jnp.broadcast_to(inverse, (BLK, HD))
        qrot[rows, :] = rotate(unit * gain_q, ctab[0], stab[0]).astype(BF16)
        d = qod[2, :, lanes]
        dor[rows, :] = d
        prod = d.astype(F32) * qod[1, :, lanes].astype(F32)
        delta[:, lanes] = jnp.sum(prod.T, axis=0, keepdims=True)

    for n in range(2):
        kv_arrived(2, (n,))
        send(kv_copy(n, 2, 4, at(2)))
        send(kv_copy(n, 2, 3 - 2 * c, partner))
    sum_wait(zr, 2 * JUMP, r_zr.at[0])
    for j in range(1, JUMP + 1):
        zr_send(1, z_at(-j), z_at(JUMP))
        if j < JUMP:
            zr_send(1, z_at(j), z_at(-JUMP))

    def to_rows(n):
        x = pqod[n].astype(F32)
        for g in range(G):
            scr[2 * g : 2 * g + 2, :] = x[:, g * HD : (g + 1) * HD]
        return scr[0:16, :]

    pslot = gi * 32 + z * 2
    odd = lax.rem(row16, 2) == 1

    def prow(n):
        first = jnp.broadcast_to(tpr_ref[n, pl.ds(pslot, 1), :], (16, HD))
        second = jnp.broadcast_to(tpr_ref[n, pl.ds(pslot + 1, 1), :], (16, HD))
        return jnp.where(odd, second, first)

    pc16, ps16 = prow(0), prow(1)
    prest = pl.ds(ROWS + 16, PROWS - 16)
    punit, pinverse = norm(to_rows(0))
    qrot[ROWS : ROWS + 16, :] = rotate(punit * gain_q, pc16, ps16).astype(BF16)
    qrot[prest, :] = jnp.zeros((PROWS - 16, HD), BF16)
    pd = to_rows(2)
    dor[ROWS : ROWS + 16, :] = pd.astype(BF16)
    dor[prest, :] = jnp.zeros((PROWS - 16, HD), BF16)
    pscr[...] = jnp.zeros((PROWS, HD), F32)
    pscr[0:16, :] = pd * to_rows(1)
    delta[:, ROWS:] = jnp.sum(pscr[...].T, axis=0, keepdims=True)

    tot[...] = jnp.zeros((1, ALLR), F32)
    dqt[...] = jnp.zeros((HD, ALLR), F32)

    def attend(krows, vals, width, visible):
        s = nt(krot[krows, :], qrot[0:width, :])
        e = jnp.where(visible, jnp.exp2(s * EXP2_SCALE), 0.0)
        tot[:, 0:width] += jnp.sum(e, axis=0, keepdims=True)
        eh[krows, 0:width] = e.astype(BF16)
        dp = nt(vals(), dor[0:width, :])
        ds = (e * (dp - delta[:, 0:width])).astype(BF16)
        dsb[krows, 0:width] = ds
        dqt[:, 0:width] += nn(krott[:, krows], ds)

    def key_block(d):
        rows = slice(PFX + d * BLK, PFX + (d + 1) * BLK)
        unit, inverse = norm(kv[d, 0].astype(F32))
        if d == 0:
            kinv[...] = jnp.broadcast_to(inverse, (BLK, HD))
        kunit[rows, :] = unit
        rot = rotate(unit * gain_k, ctab[d], stab[d])
        krot[rows, :] = rot.astype(BF16)
        krott[:, rows] = rot.T.astype(BF16)

    def wide(x):
        return jnp.concatenate([x] * G, axis=1)

    def window(first, count):
        for d in range(first, first + count):
            key_block(d)
        offs = lax.broadcasted_iota(jnp.int32, (BLK, ROWS), 0)
        visible = jnp.concatenate([offs <= thr[d] for d in range(first, first + count)], axis=0)
        attend(slice(PFX + first * BLK, PFX + (first + count) * BLK), lambda: kv[first : first + count, 1].reshape(count * BLK, HD), ROWS, visible)

    thr[0] = wide(lane1)
    window(0, 1)

    for n in range(2):
        kv_arrived(4, (n,))
        send(kv_copy(n, 4, 6, at(2)))
        send(kv_copy(n, 4, 5 - 2 * c, partner))

    sum_wait(parw, SUB - 1, r_par.at[0])
    block = me + PFX // BLK
    current = jnp.full((1, HD), block, jnp.int32)
    seen = [jnp.zeros((1, HD), jnp.int32) for _ in range(SUB)]
    levels = [jnp.zeros((1, HD), jnp.int32) for _ in range(SUB)]
    above = [parw[d] for d in range(SUB)]
    for step in range(SUB + 1):
        branchy = current >= PFX // BLK
        upward = jnp.zeros((1, HD), jnp.int32)
        for d in range(SUB):
            match = (current == block - d) & branchy
            seen[d] = jnp.where(match, 1, seen[d])
            levels[d] = jnp.where(match, level - step, levels[d])
            upward = jnp.where(match, above[d], upward)
        current = jnp.where(branchy, upward, current)
    fork = current
    for d in range(1, SUB):
        thr[d] = jnp.where(wide(seen[d]) == 1, BLK, -1)
        block_tables(d, levels[d])
    thr_prompt = jnp.concatenate(
        [wide(BLK * (fork + 1) - 1), me * 2 + lax.rem(lane1, 2)], axis=1
    )

    kv_arrived(1)
    window(1, 2)

    def last_hop(n):
        kv_arrived(6, (n,))
        send(kv_copy(n, 6, 7, at(1)))

        @pl.when(c == 1)
        def _():
            kv_copy(n, 6, 5, partner).start()

    for n in range(2):
        last_hop(n)

    sum_wait(zr, 2 * JUMP - 1, r_zr.at[1])
    for n in range(2):
        for k in range(Z):
            dn[n * 32 + 2 * k : n * 32 + 2 * k + 2, :] = zr[k, n].astype(F32)
    grp[0, gi] = dn[0:32, :].astype(BF16)
    grp[1, gi] = dn[32:64, :].astype(BF16)
    kv_arrived(3)
    for n in range(2):
        for j in range(1, GRP):
            other = grp_dev(lax.rem(gi + j, GRP))
            send(copy(grp.at[n, gi], grp.at[n, gi], s_ag2.at[n], r_ag2.at[n], other))
    window(3, 2)
    kv_arrived(5)
    kv_arrived(7)
    window(5, 3)

    def grp_arrived(n):
        sum_wait(grp.at[n], GRP - 1, r_ag2.at[n])

    grp_arrived(0)
    pcos, psin = tpr_ref[0], tpr_ref[1]
    pk_all = grp[0].reshape(PFX, HD).astype(F32)
    pkunit, _ = norm(pk_all)
    rot = rotate(pkunit * gain_k, pcos, psin)
    krot[0:PFX, :] = rot.astype(BF16)
    krott[:, 0:PFX] = rot.T.astype(BF16)
    kunit[0:PFX, :] = pkunit
    p_key = lax.broadcasted_iota(jnp.int32, (PFX, ALLR), 0)
    t_key = ((p_key >> 6) << 6) + (((p_key >> 1) & 15) << 2) + (((p_key >> 5) & 1) << 1) + (p_key & 1)

    def prompt_values():
        grp_arrived(1)
        return grp[1].reshape(PFX, HD)

    attend(slice(0, PFX), prompt_values, ALLR, t_key <= thr_prompt)

    tot[...] = 1.0 / tot[...]
    for g in range(G + 1):
        rows = slice(g * BLK, (g + 1) * BLK)
        column = jnp.broadcast_to(tot[:, rows], (BLK, BLK)).T
        qs[rows, :] = (qrot[rows, :].astype(F32) * column).astype(BF16)
        dos[rows, :] = (dor[rows, :].astype(F32) * column).astype(BF16)

    def key_grads(krows, width):
        dk = nn(dsb[krows, 0:width], qs[0:width, :]) * SCALE
        return dk, nn(eh[krows, 0:width], dos[0:width, :])

    dk, dv = key_grads(slice(0, PFX), ALLR)
    for n in range(GRP):
        pterm[n, 0:32, :] = dk[n * 32 : (n + 1) * 32].astype(BF16)
        pterm[n, 32:64, :] = dv[n * 32 : (n + 1) * 32].astype(BF16)
    gk = jnp.sum(unrotate(dk, pcos, psin) * kunit[0:PFX, :], axis=0, keepdims=True)
    for j in range(1, GRP):
        other = lax.rem(gi + j, GRP)
        send(copy(pterm.at[other], rs1.at[gi], s_rs1.at[0], r_rs1.at[0], grp_dev(other)))

    dk, dv = key_grads(slice(PFX, KEYS), ROWS)
    for d in range(SUB - 1, -1, -1):
        rows = slice(d * BLK, (d + 1) * BLK)
        if d:
            wterm[d, 0] = dk[rows].astype(BF16)
            wterm[d, 1] = dv[rows].astype(BF16)
        else:
            ownk[...] = dk[rows]
            ownv[...] = dv[rows]
        g_part = unrotate(dk[rows], ctab[d], stab[d]) * kunit[PFX + d * BLK : PFX + (d + 1) * BLK, :]
        gk = gk + jnp.sum(g_part, axis=0, keepdims=True)
    for n in range(2):
        send(copy(wterm.at[7, n], prx.at[3, n], s_p.at[0], r_p.at[0], at(-1)))
    for slot in (2, 1, 0):
        for n in range(2):
            send(copy(wterm.at[2 * slot + 1, n], prx.at[slot, n], s_p.at[0], r_p.at[0], partner))

    gq = jnp.zeros((1, HD), F32)
    for g in range(G):
        rows = slice(g * BLK, (g + 1) * BLK)
        grad = (dqt[:, rows] * (tot[:, rows] * SCALE)).T
        raw, part = norm_back(grad, qunit[rows, :], qinv[rows, :], gain_q, ctab[0], stab[0])
        dq_ref[:, rows] = raw.astype(BF16)
        gq = gq + part
    grad = (dqt[:, ROWS:] * (tot[:, ROWS:] * SCALE)).T[0:16]
    raw, part = norm_back(grad, punit, pinverse, gain_q, pc16, ps16)
    gq = gq + part
    g1[z] = jnp.concatenate([gq, gk], axis=0)
    scr[...] = raw
    for g in range(G):
        pdq_ref[:, g * HD : (g + 1) * HD] = scr[2 * g : 2 * g + 2, :].astype(BF16)

    @pl.loop(1, Z)
    def _(j):
        copy(g1.at[z], g1.at[z], s_g1.at[0], r_g1.at[0], z_dev(lax.rem(z + j, Z))).start()

    out = pltpu.make_async_copy(dq_ref, dq_hbm, s_loc.at[8])
    out.start()

    def m_arrived(k, n):
        copy(mrx.at[k, n], mrx.at[k, n], s_m.at[0], r_m.at[k, n], partner).wait_recv()

    def step_down(k):
        for n in range(2):
            if k < 3:
                m_arrived(k, n)
            value = wterm[2 * k, n].astype(F32) + prx[k - c, n].astype(F32)
            if k == 3:
                value = value + jnp.where(c == 1, prx[3, n].astype(F32), 0.0)
            else:
                value = value + mrx[k, n].astype(F32)
            mtx[k - 1, n] = value.astype(BF16)
        for n in range(2):
            send(copy(mtx.at[k - 1, n], mrx.at[k - 1, n], s_m.at[0], r_m.at[k - 1, n], at(-2)))

    sum_wait(prx, 4, r_p.at[0])
    step_down(3)

    sum_wait(rs1, GRP - 1, r_rs1.at[0])
    rs1[gi] = pterm[gi]
    total = rs1[0].astype(F32)
    for n in range(1, GRP):
        total = total + rs1[n].astype(F32)
    dn[...] = total
    for n in range(2):
        for k in range(Z):
            rs2t[k, n] = dn[n * 32 + 2 * k : n * 32 + 2 * k + 2, :].astype(BF16)
    rs2[z] = rs2t[z]

    @pl.loop(1, Z)
    def _(j):
        other = lax.rem(z + j, Z)
        copy(rs2t.at[other], rs2.at[z], s_rs2.at[0], r_rs2.at[0], z_dev(other)).start()

    step_down(2)

    sum_wait(g1, Z - 1, r_g1.at[0])
    total = g1[0]
    for n in range(1, Z):
        total = total + g1[n]
    xg = hx * GRP + gi
    g2[xg] = total

    @pl.loop(1, GRP * X)
    def _(j):
        other = lax.rem(xg + j, GRP * X)
        copy(
            g2.at[xg], g2.at[xg], s_g2.at[0], r_g2.at[0], grp_dev(lax.rem(other, GRP)), other // GRP
        ).start()

    step_down(1)

    for n, total_ref in ((0, ownk), (1, ownv)):
        m_arrived(0, n)
        total_ref[...] += mrx[0, n].astype(F32)

        @pl.when(c == 0)
        def _():
            total_ref[...] += prx[0, n].astype(F32)

    raw, _ = norm_back(
        ownk[...], kunit[PFX : PFX + BLK, :], kinv[...], gain_k, ctab[0], stab[0]
    )
    dk_ref[...] = raw.astype(BF16)
    dv_ref[...] = ownv[...].astype(BF16)

    sum_wait(rs2, Z - 1, r_rs2.at[0])
    ptk, ptv = rs2[0, 0].astype(F32), rs2[0, 1].astype(F32)
    for n in range(1, Z):
        ptk = ptk + rs2[n, 0].astype(F32)
        ptv = ptv + rs2[n, 1].astype(F32)
    unit2, inverse2 = norm(zr[z, 0].astype(F32))
    raw, _ = norm_back(ptk, unit2, inverse2, gain_k, pc16[0:2], ps16[0:2])
    pdk_ref[...] = raw.astype(BF16)
    pdv_ref[...] = ptv.astype(BF16)

    sum_wait(g2, GRP * X - 1, r_g2.at[0])
    total = g2[0]
    for n in range(1, GRP * X):
        total = total + g2[n]
    count = (NCTX * (BLK + 2)) * X
    row2 = lax.broadcasted_iota(jnp.int32, (2, HD), 0)
    factor = jnp.where(row2 == 0, (count * G) ** (-0.5), count ** (-0.5))
    gg_ref[...] = total * factor

    out.wait()
    sent(zr, 4 * JUMP - 1, s_zr.at[0])
    sent(parw, SUB - 1, s_par.at[0])
    sent(kv, 7, s_kv.at[0])
    for n in range(2):
        sent(grp.at[n], GRP - 1, s_ag2.at[n])
    sent(rs1, GRP - 1, s_rs1.at[0])
    sent(prx, 4, s_p.at[0])
    sent(mrx, 3, s_m.at[0])
    sent(rs2, Z - 1, s_rs2.at[0])
    sent(g1, Z - 1, s_g1.at[0])
    sent(g2, GRP * X - 1, s_g2.at[0])


def finish(*refs):
    count = len(refs) // 2
    for src, dst in zip(refs[:count], refs[count:]):
        dst[...] = src[...]


def per_device(
    branch_q, branch_k, branch_v, branch_o, branch_dout,
    prompt_q, prompt_k, prompt_v, prompt_o, prompt_dout, gains, parents, depth,
):
    offset, level, prompt = tables()
    vmem = pl.BlockSpec(memory_space=pltpu.VMEM)
    hbm = pl.BlockSpec(memory_space=pl.ANY)
    dma = pltpu.SemaphoreType.DMA
    vm = pltpu.VMEM
    outs = pl.pallas_call(
        kernel,
        out_shape=(
            jax.ShapeDtypeStruct((BLK, G * HD), BF16),
            jax.ShapeDtypeStruct((BLK, HD), BF16),
            jax.ShapeDtypeStruct((BLK, HD), BF16),
            jax.ShapeDtypeStruct((2, G * HD), BF16),
            jax.ShapeDtypeStruct((2, HD), BF16),
            jax.ShapeDtypeStruct((2, HD), BF16),
            jax.ShapeDtypeStruct((2, HD), F32),
        ),
        in_specs=[hbm] * 14,
        out_specs=(hbm,) + (vmem,) * 6,
        scratch_shapes=[
            vm((3, BLK, G * HD), BF16),
            vm((3, 2, G * HD), BF16),
            vm((2, BLK + 16 + PFX, HD), F32),
            vm((BLK, G * HD), BF16),
            vm((2, HD), F32),
            vm((1, 1), jnp.int32),
            vm((1, HD), jnp.int32),
            vm((SUB, 2, BLK, HD), BF16),
            vm((SUB, 1, HD), jnp.int32),
            vm((Z, 2, 2, HD), BF16),
            vm((2, GRP, 32, HD), BF16),
            vm((ALLR, HD), BF16),
            vm((ROWS, HD), F32),
            vm((ROWS, HD), F32),
            vm((ALLR, HD), BF16),
            vm((1, ALLR), F32),
            vm((KEYS, HD), BF16),
            vm((HD, KEYS), BF16),
            vm((KEYS, HD), F32),
            vm((BLK, HD), F32),
            vm((SUB, BLK, HD), F32),
            vm((SUB, BLK, HD), F32),
            vm((SUB, 1, ROWS), jnp.int32),
            vm((KEYS, ALLR), BF16),
            vm((KEYS, ALLR), BF16),
            vm((1, ALLR), F32),
            vm((HD, ALLR), F32),
            vm((ALLR, HD), BF16),
            vm((ALLR, HD), BF16),
            vm((16, HD), F32),
            vm((PROWS, HD), F32),
            vm((64, HD), F32),
            vm((SUB, 2, BLK, HD), BF16),
            vm((BLK, HD), F32),
            vm((BLK, HD), F32),
            vm((4, 2, BLK, HD), BF16),
            vm((3, 2, BLK, HD), BF16),
            vm((3, 2, BLK, HD), BF16),
            vm((GRP, 64, HD), BF16),
            vm((GRP, 64, HD), BF16),
            vm((Z, 2, 2, HD), BF16),
            vm((Z, 2, 2, HD), BF16),
            vm((Z, 2, HD), F32),
            vm((GRP * X, 2, HD), F32),
            dma((9,)),
            dma((1,)), dma((SUB, 2)),
            dma((1,)), dma((1,)),
            dma((1,)), dma((2,)),
            dma((2,)), dma((2,)),
            dma((1,)), dma((1,)),
            dma((1,)), dma((3, 2)),
            dma((1,)), dma((1,)),
            dma((1,)), dma((1,)),
            dma((1,)), dma((1,)),
            dma((1,)), dma((1,)),
        ],
        compiler_params=pltpu.CompilerParams(
            collective_id=0, has_side_effects=True, vmem_limit_bytes=60 * 1024 * 1024
        ),
        name="tree_back",
    )(
        branch_q[:, 0], branch_k[:, 0], branch_v[:, 0], branch_o[:, 0], branch_dout[:, 0],
        prompt_q[:, 0], prompt_k[:, 0], prompt_v[:, 0], prompt_o[:, 0], prompt_dout[:, 0],
        gains, parents.reshape(1, 1), depth.reshape(1, BLK),
        jnp.asarray(np.concatenate([offset, level, prompt], axis=1)),
    )
    outs = pl.pallas_call(
        finish,
        out_shape=tuple(jax.ShapeDtypeStruct(x.shape, x.dtype) for x in outs),
        in_specs=[vmem] * 7,
        out_specs=(vmem,) * 7,
        name="finish",
    )(*outs)
    dq, dk, dv, pdq, pdk, pdv, gain_grads = outs
    return (
        dq[:, None], dk[:, None], dv[:, None], pdq[:, None], pdk[:, None], pdv[:, None], gain_grads,
    )


def solution(mesh):
    tok = P("ctx", "head", None)
    return jax.shard_map(
        per_device,
        mesh=mesh,
        in_specs=(tok,) * 10 + (P(), P("ctx"), P("ctx")),
        out_specs=(tok,) * 6 + (P(),),
        check_vma=False,
    )
```

```python
import math

import numpy as np

import jax
import jax.numpy as jnp
from jax import lax
from jax.experimental import pallas as pl
from jax.experimental.pallas import tpu as pltpu
from jax.sharding import PartitionSpec as P

HD = 128
G = 8
BLK = 128
SUB = 8
PFX = 256
EPS = 1e-06
THETA = 1000000.0
Y = 4
Z = 16
GRP = 2 * Y
X = 4
JUMP = 4
NCTX = Y * Z * 2
ROWS = BLK * G
PROWS = 128
ALLR = ROWS + PROWS
KEYS = PFX + SUB * BLK
SCALE = HD ** (-0.5)
EXP2_SCALE = SCALE * math.log2(math.e)
MESH = pl.DeviceIdType.MESH
F32 = jnp.float32
BF16 = jnp.bfloat16


def prompt_order():
    p = np.arange(PFX)
    return (p // 64) * 64 + (p // 2 % Z) * 4 + (p // 32 % 2) * 2 + p % 2


def tables():
    freq = THETA ** (-(np.arange(HD // 2, dtype=np.float64) * 2.0) / HD)

    def pair(positions):
        angle = positions[:, None].astype(np.float64) * freq[None, :]
        cosine, sine = np.cos(angle), np.sin(angle)
        return np.stack(
            [np.concatenate([cosine, cosine], 1), np.concatenate([-sine, sine], 1)]
        ).astype(np.float32)

    offset = pair(np.arange(BLK))
    level = pair(np.arange(16) * BLK)
    prompt = pair(prompt_order())
    return offset, level, prompt


def norm(x):
    inverse = lax.rsqrt(jnp.mean(x * x, axis=-1, keepdims=True) + EPS)
    return x * inverse, inverse


def swap(x):
    return pltpu.roll(x, HD // 2, 1)


def rotate(x, c, s):
    return x * c + swap(x) * s


def unrotate(x, c, s):
    return x * c - swap(x) * s


def norm_back(grad, unit, inverse, gain, c, s):
    g = unrotate(grad, c, s)
    u = g * gain
    raw = (u - unit * jnp.mean(u * unit, axis=-1, keepdims=True)) * inverse
    return raw, jnp.sum(g * unit, axis=0, keepdims=True)


def nt(a, b):
    return lax.dot_general(a, b, (((1,), (1,)), ((), ())), preferred_element_type=F32)


def nn(a, b):
    return lax.dot_general(a, b, (((1,), (0,)), ((), ())), preferred_element_type=F32)


def kernel(
    q_hbm, k_hbm, v_hbm, o_hbm, do_hbm, pq_hbm, pk_hbm, pv_hbm, po_hbm, pdo_hbm,
    gains_hbm, par_hbm, depth_hbm, tab_hbm,
    dq_hbm, dk_ref, dv_ref, pdq_ref, pdk_ref, pdv_ref, gg_ref,
    qod, pqod, tab, dq_ref, gains_ref, par_ref, depth_ref,
    kv, parw, zr, grp,
    qrot, qunit, qinv, dor, delta, krot, krott, kunit, kinv, ctab, stab, thr, eh, dsb, tot, dqt,
    qs, dos, scr, pscr, dn,
    wterm, ownk, ownv, prx, mtx, mrx, pterm, rs1, rs2t, rs2, g1, g2,
    s_loc, s_kv, r_kv, s_par, r_par, s_zr, r_zr, s_ag2, r_ag2,
    s_p, r_p, s_m, r_m, s_rs1, r_rs1, s_rs2, r_rs2, s_g1, r_g1, s_g2, r_g2,
):
    me = lax.axis_index("ctx")
    hx = lax.axis_index("head")
    y = me // (2 * Z)
    z = lax.rem(me // 2, Z)
    c = lax.rem(me, 2)
    gi = y * 2 + c
    partner = me + 1 - 2 * c

    def at(offset):
        return lax.rem(me + (offset + NCTX), NCTX)

    def grp_dev(index):
        return ((index // 2) * Z + z) * 2 + lax.rem(index, 2)

    def z_dev(index):
        return (y * Z + index) * 2 + c

    def z_at(offset):
        return lax.rem(z + (offset + Z), Z)

    def copy(src, dst, ssem, rsem, device, head=None):
        where = {"ctx": device} if head is None else {"ctx": device, "head": head}
        return pltpu.make_async_remote_copy(
            src_ref=src, dst_ref=dst, send_sem=ssem, recv_sem=rsem,
            device_id=where, device_id_type=MESH,
        )

    barrier = pltpu.get_barrier_semaphore()

    def greet(device, head=None):
        where = {"ctx": device} if head is None else {"ctx": device, "head": head}
        pl.semaphore_signal(barrier, inc=1, device_id=where, device_id_type=MESH)

    for offset in (-7, -6, -5, -4, -3, -2, -1, 1, 2):
        greet(at(offset))
    for offset in range(1, JUMP + 1):
        greet(z_dev(z_at(offset)))
        greet(z_dev(z_at(-offset)))

    @pl.loop(1, GRP * X)
    def _(j):
        other = lax.rem(hx * GRP + gi + j, GRP * X)
        greet(grp_dev(lax.rem(other, GRP)), other // GRP)

    def fetch(n, src, dst):
        cp = pltpu.make_async_copy(src, dst, s_loc.at[n])
        cp.start()
        return cp

    par_in = fetch(0, par_hbm, par_ref)
    fetch(1, pk_hbm, zr.at[z, 0])
    fetch(1, pv_hbm, zr.at[z, 1])
    fetch(2, k_hbm, kv.at[0, 0])
    fetch(2, v_hbm, kv.at[0, 1])
    later = [fetch(3, gains_hbm, gains_ref), fetch(4, depth_hbm, depth_ref), fetch(5, tab_hbm, tab)]
    for n, (big, small) in enumerate(((q_hbm, pq_hbm), (o_hbm, po_hbm), (do_hbm, pdo_hbm))):
        fetch(6, big, qod.at[n])
        fetch(7, small, pqod.at[n])
    toff_ref = tab.at[:, 0:BLK]
    tlev_ref = tab.at[:, BLK : BLK + 16]
    tpr_ref = tab.at[:, BLK + 16 :]

    def fetched(n, ref):
        pltpu.make_async_copy(ref, ref, s_loc.at[n]).wait()

    par_in.wait()
    fetched(1, zr.at[z])
    fetched(2, kv.at[0])
    parw[0] = jnp.broadcast_to(par_ref[...], (1, HD))
    pl.semaphore_wait(barrier, 9 + 2 * JUMP + (GRP * X - 1))

    def kv_copy(n, src, dst, device):
        return copy(kv.at[src, n], kv.at[dst, n], s_kv.at[0], r_kv.at[dst, n], device)

    def kv_arrived(slot, halves=(0, 1)):
        for n in halves:
            copy(kv.at[slot, n], kv.at[slot, n], s_kv.at[0], r_kv.at[slot, n], partner).wait_recv()

    def send(cp):
        cp.start()

    def sum_wait(ref, count, sem):
        part = ref.at[pl.ds(0, count)]
        copy(part, part, sem, sem, partner).wait_recv()

    def sent(ref, count, sem):
        part = ref.at[pl.ds(0, count)]
        copy(part, part, sem, sem, partner).wait_send()

    def zr_send(far, slot, to):
        copy(zr.at[slot], zr.at[slot], s_zr.at[0], r_zr.at[far], z_dev(to)).start()

    for j in range(JUMP, 0, -1):
        zr_send(0, z, z_at(j))
        zr_send(0, z, z_at(-j))
    for d in range(1, SUB):
        send(copy(parw.at[0], parw.at[d], s_par.at[0], r_par.at[0], at(d)))
    for n in range(2):
        send(kv_copy(n, 0, 2, at(2)))

    @pl.when(c == 0)
    def _():
        for n in range(2):
            kv_copy(n, 0, 1, partner).start()

    row16 = lax.broadcasted_iota(jnp.int32, (16, HD), 0)
    for cp in later:
        cp.wait()
    fetched(6, qod)
    fetched(7, pqod)
    gain_q = gains_ref[0:1, :]
    gain_k = gains_ref[1:2, :]
    lane1 = lax.broadcasted_iota(jnp.int32, (1, HD), 1)
    level = (depth_ref[...] - lane1) >> 7

    def level_rows(lv):
        cl = jnp.zeros((1, HD), F32)
        sl = jnp.zeros((1, HD), F32)
        for n in range(1, SUB + 2):
            cl = jnp.where(lv == n, tlev_ref[0, n : n + 1, :], cl)
            sl = jnp.where(lv == n, tlev_ref[1, n : n + 1, :], sl)
        return cl, sl

    def block_tables(d, lv):
        cl, sl = level_rows(lv)
        co, so = toff_ref[0], toff_ref[1]
        ctab[d] = co * cl - so * sl
        stab[d] = so * cl + co * sl

    block_tables(0, level)

    @pl.loop(0, G)
    def _(g):
        lanes = pl.ds(pl.multiple_of(g * HD, HD), HD)
        rows = pl.ds(pl.multiple_of(g * BLK, BLK), BLK)
        unit, inverse = norm(qod[0, :, lanes].astype(F32))
        qunit[rows, :] = unit
        qinv[rows, :] = jnp.broadcast_to(inverse, (BLK, HD))
        qrot[rows, :] = rotate(unit * gain_q, ctab[0], stab[0]).astype(BF16)
        d = qod[2, :, lanes]
        dor[rows, :] = d
        prod = d.astype(F32) * qod[1, :, lanes].astype(F32)
        delta[:, lanes] = jnp.sum(prod.T, axis=0, keepdims=True)

    for n in range(2):
        kv_arrived(2, (n,))
        send(kv_copy(n, 2, 4, at(2)))
        send(kv_copy(n, 2, 3 - 2 * c, partner))
    sum_wait(zr, 2 * JUMP, r_zr.at[0])
    for j in range(1, JUMP + 1):
        zr_send(1, z_at(-j), z_at(JUMP))
        if j < JUMP:
            zr_send(1, z_at(j), z_at(-JUMP))

    def to_rows(n):
        x = pqod[n].astype(F32)
        for g in range(G):
            scr[2 * g : 2 * g + 2, :] = x[:, g * HD : (g + 1) * HD]
        return scr[0:16, :]

    pslot = gi * 32 + z * 2
    odd = lax.rem(row16, 2) == 1

    def prow(n):
        first = jnp.broadcast_to(tpr_ref[n, pl.ds(pslot, 1), :], (16, HD))
        second = jnp.broadcast_to(tpr_ref[n, pl.ds(pslot + 1, 1), :], (16, HD))
        return jnp.where(odd, second, first)

    pc16, ps16 = prow(0), prow(1)
    prest = pl.ds(ROWS + 16, PROWS - 16)
    punit, pinverse = norm(to_rows(0))
    qrot[ROWS : ROWS + 16, :] = rotate(punit * gain_q, pc16, ps16).astype(BF16)
    qrot[prest, :] = jnp.zeros((PROWS - 16, HD), BF16)
    pd = to_rows(2)
    dor[ROWS : ROWS + 16, :] = pd.astype(BF16)
    dor[prest, :] = jnp.zeros((PROWS - 16, HD), BF16)
    pscr[...] = jnp.zeros((PROWS, HD), F32)
    pscr[0:16, :] = pd * to_rows(1)
    delta[:, ROWS:] = jnp.sum(pscr[...].T, axis=0, keepdims=True)

    tot[...] = jnp.zeros((1, ALLR), F32)
    dqt[...] = jnp.zeros((HD, ALLR), F32)

    def attend(krows, vals, width, visible):
        s = nt(krot[krows, :], qrot[0:width, :])
        e = jnp.where(visible, jnp.exp2(s * EXP2_SCALE), 0.0)
        tot[:, 0:width] += jnp.sum(e, axis=0, keepdims=True)
        eh[krows, 0:width] = e.astype(BF16)
        dp = nt(vals(), dor[0:width, :])
        ds = (e * (dp - delta[:, 0:width])).astype(BF16)
        dsb[krows, 0:width] = ds
        dqt[:, 0:width] += nn(krott[:, krows], ds)

    def key_block(d):
        rows = slice(PFX + d * BLK, PFX + (d + 1) * BLK)
        unit, inverse = norm(kv[d, 0].astype(F32))
        if d == 0:
            kinv[...] = jnp.broadcast_to(inverse, (BLK, HD))
        kunit[rows, :] = unit
        rot = rotate(unit * gain_k, ctab[d], stab[d])
        krot[rows, :] = rot.astype(BF16)
        krott[:, rows] = rot.T.astype(BF16)

    def wide(x):
        return jnp.concatenate([x] * G, axis=1)

    def window(first, count):
        for d in range(first, first + count):
            key_block(d)
        offs = lax.broadcasted_iota(jnp.int32, (BLK, ROWS), 0)
        visible = jnp.concatenate([offs <= thr[d] for d in range(first, first + count)], axis=0)
        attend(slice(PFX + first * BLK, PFX + (first + count) * BLK), lambda: kv[first : first + count, 1].reshape(count * BLK, HD), ROWS, visible)

    thr[0] = wide(lane1)
    window(0, 1)

    for n in range(2):
        kv_arrived(4, (n,))
        send(kv_copy(n, 4, 6, at(2)))
        send(kv_copy(n, 4, 5 - 2 * c, partner))

    sum_wait(parw, SUB - 1, r_par.at[0])
    block = me + PFX // BLK
    current = jnp.full((1, HD), block, jnp.int32)
    seen = [jnp.zeros((1, HD), jnp.int32) for _ in range(SUB)]
    levels = [jnp.zeros((1, HD), jnp.int32) for _ in range(SUB)]
    above = [parw[d] for d in range(SUB)]
    for step in range(SUB + 1):
        branchy = current >= PFX // BLK
        upward = jnp.zeros((1, HD), jnp.int32)
        for d in range(SUB):
            match = (current == block - d) & branchy
            seen[d] = jnp.where(match, 1, seen[d])
            levels[d] = jnp.where(match, level - step, levels[d])
            upward = jnp.where(match, above[d], upward)
        current = jnp.where(branchy, upward, current)
    fork = current
    for d in range(1, SUB):
        thr[d] = jnp.where(wide(seen[d]) == 1, BLK, -1)
        block_tables(d, levels[d])
    thr_prompt = jnp.concatenate(
        [wide(BLK * (fork + 1) - 1), me * 2 + lax.rem(lane1, 2)], axis=1
    )

    kv_arrived(1)
    window(1, 2)

    sum_wait(zr, 2 * JUMP - 1, r_zr.at[1])
    for n in range(2):
        for k in range(Z):
            dn[n * 32 + 2 * k : n * 32 + 2 * k + 2, :] = zr[k, n].astype(F32)
    grp[0, gi] = dn[0:32, :].astype(BF16)
    grp[1, gi] = dn[32:64, :].astype(BF16)
    for n in range(2):
        for j in range(1, GRP):
            other = grp_dev(lax.rem(gi + j, GRP))
            send(copy(grp.at[n, gi], grp.at[n, gi], s_ag2.at[n], r_ag2.at[n], other))
    def last_hop(n):
        kv_arrived(6, (n,))
        send(kv_copy(n, 6, 7, at(1)))

        @pl.when(c == 1)
        def _():
            kv_copy(n, 6, 5, partner).start()

    for n in range(2):
        last_hop(n)

    kv_arrived(3)
    window(3, 2)
    kv_arrived(5)
    kv_arrived(7)
    window(5, 3)

    def grp_arrived(n):
        sum_wait(grp.at[n], GRP - 1, r_ag2.at[n])

    grp_arrived(0)
    pcos, psin = tpr_ref[0], tpr_ref[1]
    pk_all = grp[0].reshape(PFX, HD).astype(F32)
    pkunit, _ = norm(pk_all)
    rot = rotate(pkunit * gain_k, pcos, psin)
    krot[0:PFX, :] = rot.astype(BF16)
    krott[:, 0:PFX] = rot.T.astype(BF16)
    kunit[0:PFX, :] = pkunit
    p_key = lax.broadcasted_iota(jnp.int32, (PFX, ALLR), 0)
    t_key = ((p_key >> 6) << 6) + (((p_key >> 1) & 15) << 2) + (((p_key >> 5) & 1) << 1) + (p_key & 1)

    def prompt_values():
        grp_arrived(1)
        return grp[1].reshape(PFX, HD)

    attend(slice(0, PFX), prompt_values, ALLR, t_key <= thr_prompt)

    tot[...] = 1.0 / tot[...]
    for g in range(G + 1):
        rows = slice(g * BLK, (g + 1) * BLK)
        column = jnp.broadcast_to(tot[:, rows], (BLK, BLK)).T
        qs[rows, :] = (qrot[rows, :].astype(F32) * column).astype(BF16)
        dos[rows, :] = (dor[rows, :].astype(F32) * column).astype(BF16)

    def key_grads(krows, width):
        dk = nn(dsb[krows, 0:width], qs[0:width, :]) * SCALE
        return dk, nn(eh[krows, 0:width], dos[0:width, :])

    dk, dv = key_grads(slice(0, PFX), ALLR)
    for n in range(GRP):
        pterm[n, 0:32, :] = dk[n * 32 : (n + 1) * 32].astype(BF16)
        pterm[n, 32:64, :] = dv[n * 32 : (n + 1) * 32].astype(BF16)
    gk = jnp.sum(unrotate(dk, pcos, psin) * kunit[0:PFX, :], axis=0, keepdims=True)
    for j in range(1, GRP):
        other = lax.rem(gi + j, GRP)
        send(copy(pterm.at[other], rs1.at[gi], s_rs1.at[0], r_rs1.at[0], grp_dev(other)))

    def window_grads(first, last):
        dk, dv = key_grads(slice(PFX + first * BLK, PFX + (last + 1) * BLK), ROWS)
        part = jnp.zeros((1, HD), F32)
        for d in range(last, first - 1, -1):
            rows = slice((d - first) * BLK, (d - first + 1) * BLK)
            if d:
                wterm[d, 0] = dk[rows].astype(BF16)
                wterm[d, 1] = dv[rows].astype(BF16)
            else:
                ownk[...] = dk[rows]
                ownv[...] = dv[rows]
            keys = slice(PFX + d * BLK, PFX + (d + 1) * BLK)
            part = part + jnp.sum(unrotate(dk[rows], ctab[d], stab[d]) * kunit[keys, :], axis=0, keepdims=True)
        return part

    def term_out(slot):
        for n in range(2):
            device = partner if slot < 3 else at(-1)
            send(copy(wterm.at[2 * slot + 1, n], prx.at[slot, n], s_p.at[0], r_p.at[slot // 2], device))

    gk = gk + window_grads(5, 7)
    term_out(3)
    term_out(2)
    gk = gk + window_grads(0, 4)
    term_out(1)
    term_out(0)

    gq = jnp.zeros((1, HD), F32)
    for g in range(G):
        rows = slice(g * BLK, (g + 1) * BLK)
        grad = (dqt[:, rows] * (tot[:, rows] * SCALE)).T
        raw, part = norm_back(grad, qunit[rows, :], qinv[rows, :], gain_q, ctab[0], stab[0])
        dq_ref[:, rows] = raw.astype(BF16)
        gq = gq + part
    grad = (dqt[:, ROWS:] * (tot[:, ROWS:] * SCALE)).T[0:16]
    raw, part = norm_back(grad, punit, pinverse, gain_q, pc16, ps16)
    gq = gq + part
    g1[z] = jnp.concatenate([gq, gk], axis=0)
    scr[...] = raw
    for g in range(G):
        pdq_ref[:, g * HD : (g + 1) * HD] = scr[2 * g : 2 * g + 2, :].astype(BF16)

    @pl.loop(1, Z)
    def _(j):
        copy(g1.at[z], g1.at[z], s_g1.at[0], r_g1.at[0], z_dev(lax.rem(z + j, Z))).start()

    out = pltpu.make_async_copy(dq_ref, dq_hbm, s_loc.at[8])
    out.start()

    def m_arrived(k, n):
        copy(mrx.at[k, n], mrx.at[k, n], s_m.at[0], r_m.at[k, n], partner).wait_recv()

    def step_down(k):
        for n in range(2):
            if k < 3:
                m_arrived(k, n)
            value = wterm[2 * k, n].astype(F32) + prx[k - c, n].astype(F32)
            if k == 3:
                value = value + jnp.where(c == 1, prx[3, n].astype(F32), 0.0)
            else:
                value = value + mrx[k, n].astype(F32)
            mtx[k - 1, n] = value.astype(BF16)
            send(copy(mtx.at[k - 1, n], mrx.at[k - 1, n], s_m.at[0], r_m.at[k - 1, n], at(-2)))

    sum_wait(prx, 2, r_p.at[1])
    step_down(3)
    sum_wait(prx, 2, r_p.at[0])

    sum_wait(rs1, GRP - 1, r_rs1.at[0])
    rs1[gi] = pterm[gi]
    total = rs1[0].astype(F32)
    for n in range(1, GRP):
        total = total + rs1[n].astype(F32)
    dn[...] = total
    for n in range(2):
        for k in range(Z):
            rs2t[k, n] = dn[n * 32 + 2 * k : n * 32 + 2 * k + 2, :].astype(BF16)
    rs2[z] = rs2t[z]

    @pl.loop(1, Z)
    def _(j):
        other = lax.rem(z + j, Z)
        copy(rs2t.at[other], rs2.at[z], s_rs2.at[0], r_rs2.at[0], z_dev(other)).start()

    step_down(2)

    sum_wait(g1, Z - 1, r_g1.at[0])
    total = g1[0]
    for n in range(1, Z):
        total = total + g1[n]
    xg = hx * GRP + gi
    g2[xg] = total

    @pl.loop(1, GRP * X)
    def _(j):
        other = lax.rem(xg + j, GRP * X)
        copy(
            g2.at[xg], g2.at[xg], s_g2.at[0], r_g2.at[0], grp_dev(lax.rem(other, GRP)), other // GRP
        ).start()

    step_down(1)

    for n, total_ref in ((0, ownk), (1, ownv)):
        m_arrived(0, n)
        total_ref[...] += mrx[0, n].astype(F32)

        @pl.when(c == 0)
        def _():
            total_ref[...] += prx[0, n].astype(F32)

    raw, _ = norm_back(
        ownk[...], kunit[PFX : PFX + BLK, :], kinv[...], gain_k, ctab[0], stab[0]
    )
    dk_ref[...] = raw.astype(BF16)
    dv_ref[...] = ownv[...].astype(BF16)

    sum_wait(rs2, Z - 1, r_rs2.at[0])
    ptk, ptv = rs2[0, 0].astype(F32), rs2[0, 1].astype(F32)
    for n in range(1, Z):
        ptk = ptk + rs2[n, 0].astype(F32)
        ptv = ptv + rs2[n, 1].astype(F32)
    unit2, inverse2 = norm(zr[z, 0].astype(F32))
    raw, _ = norm_back(ptk, unit2, inverse2, gain_k, pc16[0:2], ps16[0:2])
    pdk_ref[...] = raw.astype(BF16)
    pdv_ref[...] = ptv.astype(BF16)

    sum_wait(g2, GRP * X - 1, r_g2.at[0])
    total = g2[0]
    for n in range(1, GRP * X):
        total = total + g2[n]
    count = (NCTX * (BLK + 2)) * X
    row2 = lax.broadcasted_iota(jnp.int32, (2, HD), 0)
    factor = jnp.where(row2 == 0, (count * G) ** (-0.5), count ** (-0.5))
    gg_ref[...] = total * factor

    out.wait()
    sent(zr, 4 * JUMP - 1, s_zr.at[0])
    sent(parw, SUB - 1, s_par.at[0])
    sent(kv, 7, s_kv.at[0])
    for n in range(2):
        sent(grp.at[n], GRP - 1, s_ag2.at[n])
    sent(rs1, GRP - 1, s_rs1.at[0])
    sent(prx, 4, s_p.at[0])
    sent(mrx, 3, s_m.at[0])
    sent(rs2, Z - 1, s_rs2.at[0])
    sent(g1, Z - 1, s_g1.at[0])
    sent(g2, GRP * X - 1, s_g2.at[0])


def finish(*refs):
    count = len(refs) // 2
    for src, dst in zip(refs[:count], refs[count:]):
        dst[...] = src[...]


def per_device(
    branch_q, branch_k, branch_v, branch_o, branch_dout,
    prompt_q, prompt_k, prompt_v, prompt_o, prompt_dout, gains, parents, depth,
):
    offset, level, prompt = tables()
    vmem = pl.BlockSpec(memory_space=pltpu.VMEM)
    hbm = pl.BlockSpec(memory_space=pl.ANY)
    dma = pltpu.SemaphoreType.DMA
    vm = pltpu.VMEM
    outs = pl.pallas_call(
        kernel,
        out_shape=(
            jax.ShapeDtypeStruct((BLK, G * HD), BF16),
            jax.ShapeDtypeStruct((BLK, HD), BF16),
            jax.ShapeDtypeStruct((BLK, HD), BF16),
            jax.ShapeDtypeStruct((2, G * HD), BF16),
            jax.ShapeDtypeStruct((2, HD), BF16),
            jax.ShapeDtypeStruct((2, HD), BF16),
            jax.ShapeDtypeStruct((2, HD), F32),
        ),
        in_specs=[hbm] * 14,
        out_specs=(hbm,) + (vmem,) * 6,
        scratch_shapes=[
            vm((3, BLK, G * HD), BF16),
            vm((3, 2, G * HD), BF16),
            vm((2, BLK + 16 + PFX, HD), F32),
            vm((BLK, G * HD), BF16),
            vm((2, HD), F32),
            vm((1, 1), jnp.int32),
            vm((1, HD), jnp.int32),
            vm((SUB, 2, BLK, HD), BF16),
            vm((SUB, 1, HD), jnp.int32),
            vm((Z, 2, 2, HD), BF16),
            vm((2, GRP, 32, HD), BF16),
            vm((ALLR, HD), BF16),
            vm((ROWS, HD), F32),
            vm((ROWS, HD), F32),
            vm((ALLR, HD), BF16),
            vm((1, ALLR), F32),
            vm((KEYS, HD), BF16),
            vm((HD, KEYS), BF16),
            vm((KEYS, HD), F32),
            vm((BLK, HD), F32),
            vm((SUB, BLK, HD), F32),
            vm((SUB, BLK, HD), F32),
            vm((SUB, 1, ROWS), jnp.int32),
            vm((KEYS, ALLR), BF16),
            vm((KEYS, ALLR), BF16),
            vm((1, ALLR), F32),
            vm((HD, ALLR), F32),
            vm((ALLR, HD), BF16),
            vm((ALLR, HD), BF16),
            vm((16, HD), F32),
            vm((PROWS, HD), F32),
            vm((64, HD), F32),
            vm((SUB, 2, BLK, HD), BF16),
            vm((BLK, HD), F32),
            vm((BLK, HD), F32),
            vm((4, 2, BLK, HD), BF16),
            vm((3, 2, BLK, HD), BF16),
            vm((3, 2, BLK, HD), BF16),
            vm((GRP, 64, HD), BF16),
            vm((GRP, 64, HD), BF16),
            vm((Z, 2, 2, HD), BF16),
            vm((Z, 2, 2, HD), BF16),
            vm((Z, 2, HD), F32),
            vm((GRP * X, 2, HD), F32),
            dma((9,)),
            dma((1,)), dma((SUB, 2)),
            dma((1,)), dma((1,)),
            dma((1,)), dma((2,)),
            dma((2,)), dma((2,)),
            dma((1,)), dma((2,)),
            dma((1,)), dma((3, 2)),
            dma((1,)), dma((1,)),
            dma((1,)), dma((1,)),
            dma((1,)), dma((1,)),
            dma((1,)), dma((1,)),
        ],
        compiler_params=pltpu.CompilerParams(
            collective_id=0, has_side_effects=True, vmem_limit_bytes=60 * 1024 * 1024
        ),
        name="tree_back",
    )(
        branch_q[:, 0], branch_k[:, 0], branch_v[:, 0], branch_o[:, 0], branch_dout[:, 0],
        prompt_q[:, 0], prompt_k[:, 0], prompt_v[:, 0], prompt_o[:, 0], prompt_dout[:, 0],
        gains, parents.reshape(1, 1), depth.reshape(1, BLK),
        jnp.asarray(np.concatenate([offset, level, prompt], axis=1)),
    )
    outs = pl.pallas_call(
        finish,
        out_shape=tuple(jax.ShapeDtypeStruct(x.shape, x.dtype) for x in outs),
        in_specs=[vmem] * 7,
        out_specs=(vmem,) * 7,
        name="finish",
    )(*outs)
    dq, dk, dv, pdq, pdk, pdv, gain_grads = outs
    return (
        dq[:, None], dk[:, None], dv[:, None], pdq[:, None], pdk[:, None], pdv[:, None], gain_grads,
    )


def solution(mesh):
    tok = P("ctx", "head", None)
    return jax.shard_map(
        per_device,
        mesh=mesh,
        in_specs=(tok,) * 10 + (P(), P("ctx"), P("ctx")),
        out_specs=(tok,) * 6 + (P(),),
        check_vma=False,
    )
```

```python
import math

import numpy as np

import jax
import jax.numpy as jnp
from jax import lax
from jax.experimental import pallas as pl
from jax.experimental.pallas import tpu as pltpu
from jax.sharding import PartitionSpec as P

HD = 128
G = 8
BLK = 128
SUB = 8
PFX = 256
EPS = 1e-06
THETA = 1000000.0
Y = 4
Z = 16
GRP = 2 * Y
X = 4
JUMP = 4
NCTX = Y * Z * 2
ROWS = BLK * G
PROWS = 128
ALLR = ROWS + PROWS
KEYS = PFX + SUB * BLK
SCALE = HD ** (-0.5)
EXP2_SCALE = SCALE * math.log2(math.e)
MESH = pl.DeviceIdType.MESH
F32 = jnp.float32
BF16 = jnp.bfloat16


def prompt_order():
    p = np.arange(PFX)
    return (p // 64) * 64 + (p // 2 % Z) * 4 + (p // 32 % 2) * 2 + p % 2


def tables():
    freq = THETA ** (-(np.arange(HD // 2, dtype=np.float64) * 2.0) / HD)

    def pair(positions):
        angle = positions[:, None].astype(np.float64) * freq[None, :]
        cosine, sine = np.cos(angle), np.sin(angle)
        return np.stack(
            [np.concatenate([cosine, cosine], 1), np.concatenate([-sine, sine], 1)]
        ).astype(np.float32)

    offset = pair(np.arange(BLK))
    level = pair(np.arange(16) * BLK)
    prompt = pair(prompt_order())
    return offset, level, prompt


def norm(x):
    inverse = lax.rsqrt(jnp.mean(x * x, axis=-1, keepdims=True) + EPS)
    return x * inverse, inverse


def swap(x):
    return pltpu.roll(x, HD // 2, 1)


def rotate(x, c, s):
    return x * c + swap(x) * s


def unrotate(x, c, s):
    return x * c - swap(x) * s


def norm_back(grad, unit, inverse, gain, c, s):
    g = unrotate(grad, c, s)
    u = g * gain
    raw = (u - unit * jnp.mean(u * unit, axis=-1, keepdims=True)) * inverse
    return raw, jnp.sum(g * unit, axis=0, keepdims=True)


def nt(a, b):
    return lax.dot_general(a, b, (((1,), (1,)), ((), ())), preferred_element_type=F32)


def nn(a, b):
    return lax.dot_general(a, b, (((1,), (0,)), ((), ())), preferred_element_type=F32)


def kernel(
    q_hbm, k_hbm, v_hbm, o_hbm, do_hbm, pq_hbm, pk_hbm, pv_hbm, po_hbm, pdo_hbm,
    gains_hbm, par_hbm, depth_hbm, tab_hbm,
    dq_hbm, dk_ref, dv_ref, pdq_ref, pdk_ref, pdv_ref, gg_ref,
    qod, pqod, tab, dq_ref, gains_ref, par_ref, depth_ref,
    kv, parw, zr, grp,
    qrot, qunit, qinv, dor, delta, krot, krott, kunit, kinv, ctab, stab, thr, eh, dsb, tot, dqt,
    qs, dos, scr, pscr, dn,
    wterm, ownk, ownv, prx, mtx, mrx, pterm, rs1, rs2t, rs2, g1, g2,
    s_loc, s_kv, r_kv, s_par, r_par, s_zr, r_zr, s_ag2, r_ag2,
    s_p, r_p, s_m, r_m, s_rs1, r_rs1, s_rs2, r_rs2, s_g1, r_g1, s_g2, r_g2,
):
    me = lax.axis_index("ctx")
    hx = lax.axis_index("head")
    y = me // (2 * Z)
    z = lax.rem(me // 2, Z)
    c = lax.rem(me, 2)
    gi = y * 2 + c
    partner = me + 1 - 2 * c

    def at(offset):
        return lax.rem(me + (offset + NCTX), NCTX)

    def grp_dev(index):
        return ((index // 2) * Z + z) * 2 + lax.rem(index, 2)

    def z_dev(index):
        return (y * Z + index) * 2 + c

    def z_at(offset):
        return lax.rem(z + (offset + Z), Z)

    def copy(src, dst, ssem, rsem, device, head=None):
        where = {"ctx": device} if head is None else {"ctx": device, "head": head}
        return pltpu.make_async_remote_copy(
            src_ref=src, dst_ref=dst, send_sem=ssem, recv_sem=rsem,
            device_id=where, device_id_type=MESH,
        )

    barrier = pltpu.get_barrier_semaphore()

    def greet(device, head=None):
        where = {"ctx": device} if head is None else {"ctx": device, "head": head}
        pl.semaphore_signal(barrier, inc=1, device_id=where, device_id_type=MESH)

    for offset in (-7, -6, -5, -4, -3, -2, -1, 1, 2):
        greet(at(offset))
    for offset in range(1, JUMP + 1):
        greet(z_dev(z_at(offset)))
        greet(z_dev(z_at(-offset)))

    @pl.loop(1, GRP * X)
    def _(j):
        other = lax.rem(hx * GRP + gi + j, GRP * X)
        greet(grp_dev(lax.rem(other, GRP)), other // GRP)

    def fetch(n, src, dst):
        cp = pltpu.make_async_copy(src, dst, s_loc.at[n])
        cp.start()
        return cp

    par_in = fetch(0, par_hbm, par_ref)
    fetch(1, pk_hbm, zr.at[z, 0])
    fetch(1, pv_hbm, zr.at[z, 1])
    fetch(2, k_hbm, kv.at[0, 0])
    fetch(2, v_hbm, kv.at[0, 1])
    later = [fetch(3, gains_hbm, gains_ref), fetch(4, depth_hbm, depth_ref), fetch(5, tab_hbm, tab)]
    for n, (big, small) in enumerate(((q_hbm, pq_hbm), (o_hbm, po_hbm), (do_hbm, pdo_hbm))):
        fetch(6, big, qod.at[n])
        fetch(7, small, pqod.at[n])
    toff_ref = tab.at[:, 0:BLK]
    tlev_ref = tab.at[:, BLK : BLK + 16]
    tpr_ref = tab.at[:, BLK + 16 :]

    def fetched(n, ref):
        pltpu.make_async_copy(ref, ref, s_loc.at[n]).wait()

    par_in.wait()
    fetched(1, zr.at[z])
    fetched(2, kv.at[0])
    parw[0] = jnp.broadcast_to(par_ref[...], (1, HD))
    pl.semaphore_wait(barrier, 9 + 2 * JUMP + (GRP * X - 1))

    def kv_copy(n, src, dst, device):
        return copy(kv.at[src, n], kv.at[dst, n], s_kv.at[0], r_kv.at[dst, n], device)

    def kv_arrived(slot, halves=(0, 1)):
        for n in halves:
            copy(kv.at[slot, n], kv.at[slot, n], s_kv.at[0], r_kv.at[slot, n], partner).wait_recv()

    def send(cp):
        cp.start()

    def sum_wait(ref, count, sem):
        part = ref.at[pl.ds(0, count)]
        copy(part, part, sem, sem, partner).wait_recv()

    def sent(ref, count, sem):
        part = ref.at[pl.ds(0, count)]
        copy(part, part, sem, sem, partner).wait_send()

    def zr_send(far, slot, to):
        copy(zr.at[slot], zr.at[slot], s_zr.at[0], r_zr.at[far], z_dev(to)).start()

    for j in range(JUMP, 0, -1):
        zr_send(0, z, z_at(j))
        zr_send(0, z, z_at(-j))
    for d in range(1, SUB):
        send(copy(parw.at[0], parw.at[d], s_par.at[0], r_par.at[0], at(d)))
    for n in range(2):
        send(kv_copy(n, 0, 2, at(2)))

    @pl.when(c == 0)
    def _():
        for n in range(2):
            kv_copy(n, 0, 1, partner).start()

    row16 = lax.broadcasted_iota(jnp.int32, (16, HD), 0)
    for cp in later:
        cp.wait()
    fetched(6, qod)
    fetched(7, pqod)
    gain_q = gains_ref[0:1, :]
    gain_k = gains_ref[1:2, :]
    lane1 = lax.broadcasted_iota(jnp.int32, (1, HD), 1)
    level = (depth_ref[...] - lane1) >> 7

    def level_rows(lv):
        cl = jnp.zeros((1, HD), F32)
        sl = jnp.zeros((1, HD), F32)
        for n in range(1, SUB + 2):
            cl = jnp.where(lv == n, tlev_ref[0, n : n + 1, :], cl)
            sl = jnp.where(lv == n, tlev_ref[1, n : n + 1, :], sl)
        return cl, sl

    def block_tables(d, lv):
        cl, sl = level_rows(lv)
        co, so = toff_ref[0], toff_ref[1]
        ctab[d] = co * cl - so * sl
        stab[d] = so * cl + co * sl

    block_tables(0, level)

    @pl.loop(0, G)
    def _(g):
        lanes = pl.ds(pl.multiple_of(g * HD, HD), HD)
        rows = pl.ds(pl.multiple_of(g * BLK, BLK), BLK)
        unit, inverse = norm(qod[0, :, lanes].astype(F32))
        qunit[rows, :] = unit
        qinv[rows, :] = jnp.broadcast_to(inverse, (BLK, HD))
        qrot[rows, :] = rotate(unit * gain_q, ctab[0], stab[0]).astype(BF16)
        d = qod[2, :, lanes]
        dor[rows, :] = d
        prod = d.astype(F32) * qod[1, :, lanes].astype(F32)
        delta[:, lanes] = jnp.sum(prod.T, axis=0, keepdims=True)

    for n in range(2):
        kv_arrived(2, (n,))
        send(kv_copy(n, 2, 4, at(2)))
        send(kv_copy(n, 2, 3 - 2 * c, partner))
    sum_wait(zr, 2 * JUMP, r_zr.at[0])
    for j in range(1, JUMP + 1):
        zr_send(1, z_at(-j), z_at(JUMP))
        if j < JUMP:
            zr_send(1, z_at(j), z_at(-JUMP))

    tot[...] = jnp.zeros((1, ALLR), F32)
    dqt[...] = jnp.zeros((HD, ALLR), F32)

    def attend(krows, vals, width, visible):
        s = nt(krot[krows, :], qrot[0:width, :])
        e = jnp.where(visible, jnp.exp2(s * EXP2_SCALE), 0.0)
        tot[:, 0:width] += jnp.sum(e, axis=0, keepdims=True)
        eh[krows, 0:width] = e.astype(BF16)
        dp = nt(vals(), dor[0:width, :])
        ds = (e * (dp - delta[:, 0:width])).astype(BF16)
        dsb[krows, 0:width] = ds
        dqt[:, 0:width] += nn(krott[:, krows], ds)

    def key_block(d):
        rows = slice(PFX + d * BLK, PFX + (d + 1) * BLK)
        unit, inverse = norm(kv[d, 0].astype(F32))
        if d == 0:
            kinv[...] = jnp.broadcast_to(inverse, (BLK, HD))
        kunit[rows, :] = unit
        rot = rotate(unit * gain_k, ctab[d], stab[d])
        krot[rows, :] = rot.astype(BF16)
        krott[:, rows] = rot.T.astype(BF16)

    def wide(x):
        return jnp.concatenate([x] * G, axis=1)

    def window(first, count):
        for d in range(first, first + count):
            key_block(d)
        offs = lax.broadcasted_iota(jnp.int32, (BLK, ROWS), 0)
        visible = jnp.concatenate([offs <= thr[d] for d in range(first, first + count)], axis=0)
        attend(slice(PFX + first * BLK, PFX + (first + count) * BLK), lambda: kv[first : first + count, 1].reshape(count * BLK, HD), ROWS, visible)

    thr[0] = wide(lane1)
    window(0, 1)

    for n in range(2):
        kv_arrived(4, (n,))
        send(kv_copy(n, 4, 6, at(2)))
        send(kv_copy(n, 4, 5 - 2 * c, partner))

    sum_wait(parw, SUB - 1, r_par.at[0])
    block = me + PFX // BLK
    current = jnp.full((1, HD), block, jnp.int32)
    seen = [jnp.zeros((1, HD), jnp.int32) for _ in range(SUB)]
    levels = [jnp.zeros((1, HD), jnp.int32) for _ in range(SUB)]
    above = [parw[d] for d in range(SUB)]
    for step in range(SUB + 1):
        branchy = current >= PFX // BLK
        upward = jnp.zeros((1, HD), jnp.int32)
        for d in range(SUB):
            match = (current == block - d) & branchy
            seen[d] = jnp.where(match, 1, seen[d])
            levels[d] = jnp.where(match, level - step, levels[d])
            upward = jnp.where(match, above[d], upward)
        current = jnp.where(branchy, upward, current)
    fork = current
    for d in range(1, SUB):
        thr[d] = jnp.where(wide(seen[d]) == 1, BLK, -1)
        block_tables(d, levels[d])
    thr_prompt = jnp.concatenate(
        [wide(BLK * (fork + 1) - 1), me * 2 + lax.rem(lane1, 2)], axis=1
    )

    kv_arrived(1)
    window(1, 2)

    sum_wait(zr, 2 * JUMP - 1, r_zr.at[1])
    for n in range(2):
        for k in range(Z):
            dn[n * 32 + 2 * k : n * 32 + 2 * k + 2, :] = zr[k, n].astype(F32)
    grp[0, gi] = dn[0:32, :].astype(BF16)
    grp[1, gi] = dn[32:64, :].astype(BF16)
    for n in range(2):
        for j in range(1, GRP):
            other = grp_dev(lax.rem(gi + j, GRP))
            send(copy(grp.at[n, gi], grp.at[n, gi], s_ag2.at[n], r_ag2.at[n], other))
    def last_hop(n):
        kv_arrived(6, (n,))
        send(kv_copy(n, 6, 7, at(1)))

        @pl.when(c == 1)
        def _():
            kv_copy(n, 6, 5, partner).start()

    for n in range(2):
        last_hop(n)

    kv_arrived(3)
    window(3, 2)
    kv_arrived(5)
    kv_arrived(7)
    window(5, 3)

    def to_rows(n):
        x = pqod[n].astype(F32)
        for g in range(G):
            scr[2 * g : 2 * g + 2, :] = x[:, g * HD : (g + 1) * HD]
        return scr[0:16, :]

    pslot = gi * 32 + z * 2
    odd = lax.rem(row16, 2) == 1

    def prow(n):
        first = jnp.broadcast_to(tpr_ref[n, pl.ds(pslot, 1), :], (16, HD))
        second = jnp.broadcast_to(tpr_ref[n, pl.ds(pslot + 1, 1), :], (16, HD))
        return jnp.where(odd, second, first)

    pc16, ps16 = prow(0), prow(1)
    prest = pl.ds(ROWS + 16, PROWS - 16)
    punit, pinverse = norm(to_rows(0))
    qrot[ROWS : ROWS + 16, :] = rotate(punit * gain_q, pc16, ps16).astype(BF16)
    qrot[prest, :] = jnp.zeros((PROWS - 16, HD), BF16)
    pd = to_rows(2)
    dor[ROWS : ROWS + 16, :] = pd.astype(BF16)
    dor[prest, :] = jnp.zeros((PROWS - 16, HD), BF16)
    pscr[...] = jnp.zeros((PROWS, HD), F32)
    pscr[0:16, :] = pd * to_rows(1)
    delta[:, ROWS:] = jnp.sum(pscr[...].T, axis=0, keepdims=True)

    def grp_arrived(n):
        sum_wait(grp.at[n], GRP - 1, r_ag2.at[n])

    grp_arrived(0)
    pcos, psin = tpr_ref[0], tpr_ref[1]
    pk_all = grp[0].reshape(PFX, HD).astype(F32)
    pkunit, _ = norm(pk_all)
    rot = rotate(pkunit * gain_k, pcos, psin)
    krot[0:PFX, :] = rot.astype(BF16)
    krott[:, 0:PFX] = rot.T.astype(BF16)
    kunit[0:PFX, :] = pkunit
    p_key = lax.broadcasted_iota(jnp.int32, (PFX, ALLR), 0)
    t_key = ((p_key >> 6) << 6) + (((p_key >> 1) & 15) << 2) + (((p_key >> 5) & 1) << 1) + (p_key & 1)

    def prompt_values():
        grp_arrived(1)
        return grp[1].reshape(PFX, HD)

    attend(slice(0, PFX), prompt_values, ALLR, t_key <= thr_prompt)

    tot[...] = 1.0 / tot[...]
    for g in range(G + 1):
        rows = slice(g * BLK, (g + 1) * BLK)
        column = jnp.broadcast_to(tot[:, rows], (BLK, BLK)).T
        qs[rows, :] = (qrot[rows, :].astype(F32) * column).astype(BF16)
        dos[rows, :] = (dor[rows, :].astype(F32) * column).astype(BF16)

    def key_grads(krows, width):
        dk = nn(dsb[krows, 0:width], qs[0:width, :]) * SCALE
        return dk, nn(eh[krows, 0:width], dos[0:width, :])

    dk, dv = key_grads(slice(0, PFX), ALLR)
    for n in range(GRP):
        pterm[n, 0:32, :] = dk[n * 32 : (n + 1) * 32].astype(BF16)
        pterm[n, 32:64, :] = dv[n * 32 : (n + 1) * 32].astype(BF16)
    gk = jnp.sum(unrotate(dk, pcos, psin) * kunit[0:PFX, :], axis=0, keepdims=True)
    for j in range(1, GRP):
        other = lax.rem(gi + j, GRP)
        send(copy(pterm.at[other], rs1.at[gi], s_rs1.at[0], r_rs1.at[0], grp_dev(other)))

    def window_grads(first, last):
        dk, dv = key_grads(slice(PFX + first * BLK, PFX + (last + 1) * BLK), ROWS)
        part = jnp.zeros((1, HD), F32)
        for d in range(last, first - 1, -1):
            rows = slice((d - first) * BLK, (d - first + 1) * BLK)
            if d:
                wterm[d, 0] = dk[rows].astype(BF16)
                wterm[d, 1] = dv[rows].astype(BF16)
            else:
                ownk[...] = dk[rows]
                ownv[...] = dv[rows]
            keys = slice(PFX + d * BLK, PFX + (d + 1) * BLK)
            part = part + jnp.sum(unrotate(dk[rows], ctab[d], stab[d]) * kunit[keys, :], axis=0, keepdims=True)
        return part

    def term_out(slot):
        for n in range(2):
            device = partner if slot < 3 else at(-1)
            send(copy(wterm.at[2 * slot + 1, n], prx.at[slot, n], s_p.at[0], r_p.at[slot // 2], device))

    gk = gk + window_grads(5, 7)
    term_out(3)
    term_out(2)
    gk = gk + window_grads(0, 4)
    term_out(1)
    term_out(0)

    gq = jnp.zeros((1, HD), F32)
    for g in range(G):
        rows = slice(g * BLK, (g + 1) * BLK)
        grad = (dqt[:, rows] * (tot[:, rows] * SCALE)).T
        raw, part = norm_back(grad, qunit[rows, :], qinv[rows, :], gain_q, ctab[0], stab[0])
        dq_ref[:, rows] = raw.astype(BF16)
        gq = gq + part
    grad = (dqt[:, ROWS:] * (tot[:, ROWS:] * SCALE)).T[0:16]
    raw, part = norm_back(grad, punit, pinverse, gain_q, pc16, ps16)
    gq = gq + part
    g1[z] = jnp.concatenate([gq, gk], axis=0)
    scr[...] = raw
    for g in range(G):
        pdq_ref[:, g * HD : (g + 1) * HD] = scr[2 * g : 2 * g + 2, :].astype(BF16)

    @pl.loop(1, Z)
    def _(j):
        copy(g1.at[z], g1.at[z], s_g1.at[0], r_g1.at[0], z_dev(lax.rem(z + j, Z))).start()

    out = pltpu.make_async_copy(dq_ref, dq_hbm, s_loc.at[8])
    out.start()

    def m_arrived(k, n):
        copy(mrx.at[k, n], mrx.at[k, n], s_m.at[0], r_m.at[k, n], partner).wait_recv()

    def step_down(k):
        for n in range(2):
            if k < 3:
                m_arrived(k, n)
            value = wterm[2 * k, n].astype(F32) + prx[k - c, n].astype(F32)
            if k == 3:
                value = value + jnp.where(c == 1, prx[3, n].astype(F32), 0.0)
            else:
                value = value + mrx[k, n].astype(F32)
            mtx[k - 1, n] = value.astype(BF16)
            send(copy(mtx.at[k - 1, n], mrx.at[k - 1, n], s_m.at[0], r_m.at[k - 1, n], at(-2)))

    sum_wait(prx, 2, r_p.at[1])
    step_down(3)
    sum_wait(prx, 2, r_p.at[0])

    sum_wait(rs1, GRP - 1, r_rs1.at[0])
    rs1[gi] = pterm[gi]
    total = rs1[0].astype(F32)
    for n in range(1, GRP):
        total = total + rs1[n].astype(F32)
    dn[...] = total
    for n in range(2):
        for k in range(Z):
            rs2t[k, n] = dn[n * 32 + 2 * k : n * 32 + 2 * k + 2, :].astype(BF16)
    rs2[z] = rs2t[z]

    @pl.loop(1, Z)
    def _(j):
        other = lax.rem(z + j, Z)
        copy(rs2t.at[other], rs2.at[z], s_rs2.at[0], r_rs2.at[0], z_dev(other)).start()

    step_down(2)

    sum_wait(g1, Z - 1, r_g1.at[0])
    total = g1[0]
    for n in range(1, Z):
        total = total + g1[n]
    xg = hx * GRP + gi
    g2[xg] = total

    @pl.loop(1, GRP * X)
    def _(j):
        other = lax.rem(xg + j, GRP * X)
        copy(
            g2.at[xg], g2.at[xg], s_g2.at[0], r_g2.at[0], grp_dev(lax.rem(other, GRP)), other // GRP
        ).start()

    step_down(1)

    for n, total_ref in ((0, ownk), (1, ownv)):
        m_arrived(0, n)
        total_ref[...] += mrx[0, n].astype(F32)

        @pl.when(c == 0)
        def _():
            total_ref[...] += prx[0, n].astype(F32)

    raw, _ = norm_back(
        ownk[...], kunit[PFX : PFX + BLK, :], kinv[...], gain_k, ctab[0], stab[0]
    )
    dk_ref[...] = raw.astype(BF16)
    dv_ref[...] = ownv[...].astype(BF16)

    sum_wait(rs2, Z - 1, r_rs2.at[0])
    ptk, ptv = rs2[0, 0].astype(F32), rs2[0, 1].astype(F32)
    for n in range(1, Z):
        ptk = ptk + rs2[n, 0].astype(F32)
        ptv = ptv + rs2[n, 1].astype(F32)
    unit2, inverse2 = norm(zr[z, 0].astype(F32))
    raw, _ = norm_back(ptk, unit2, inverse2, gain_k, pc16[0:2], ps16[0:2])
    pdk_ref[...] = raw.astype(BF16)
    pdv_ref[...] = ptv.astype(BF16)

    sum_wait(g2, GRP * X - 1, r_g2.at[0])
    total = g2[0]
    for n in range(1, GRP * X):
        total = total + g2[n]
    count = (NCTX * (BLK + 2)) * X
    row2 = lax.broadcasted_iota(jnp.int32, (2, HD), 0)
    factor = jnp.where(row2 == 0, (count * G) ** (-0.5), count ** (-0.5))
    gg_ref[...] = total * factor

    out.wait()
    sent(zr, 4 * JUMP - 1, s_zr.at[0])
    sent(parw, SUB - 1, s_par.at[0])
    sent(kv, 7, s_kv.at[0])
    for n in range(2):
        sent(grp.at[n], GRP - 1, s_ag2.at[n])
    sent(rs1, GRP - 1, s_rs1.at[0])
    sent(prx, 4, s_p.at[0])
    sent(mrx, 3, s_m.at[0])
    sent(rs2, Z - 1, s_rs2.at[0])
    sent(g1, Z - 1, s_g1.at[0])
    sent(g2, GRP * X - 1, s_g2.at[0])


def finish(*refs):
    count = len(refs) // 2
    for src, dst in zip(refs[:count], refs[count:]):
        dst[...] = src[...]


def per_device(
    branch_q, branch_k, branch_v, branch_o, branch_dout,
    prompt_q, prompt_k, prompt_v, prompt_o, prompt_dout, gains, parents, depth,
):
    offset, level, prompt = tables()
    vmem = pl.BlockSpec(memory_space=pltpu.VMEM)
    hbm = pl.BlockSpec(memory_space=pl.ANY)
    dma = pltpu.SemaphoreType.DMA
    vm = pltpu.VMEM
    outs = pl.pallas_call(
        kernel,
        out_shape=(
            jax.ShapeDtypeStruct((BLK, G * HD), BF16),
            jax.ShapeDtypeStruct((BLK, HD), BF16),
            jax.ShapeDtypeStruct((BLK, HD), BF16),
            jax.ShapeDtypeStruct((2, G * HD), BF16),
            jax.ShapeDtypeStruct((2, HD), BF16),
            jax.ShapeDtypeStruct((2, HD), BF16),
            jax.ShapeDtypeStruct((2, HD), F32),
        ),
        in_specs=[hbm] * 14,
        out_specs=(hbm,) + (vmem,) * 6,
        scratch_shapes=[
            vm((3, BLK, G * HD), BF16),
            vm((3, 2, G * HD), BF16),
            vm((2, BLK + 16 + PFX, HD), F32),
            vm((BLK, G * HD), BF16),
            vm((2, HD), F32),
            vm((1, 1), jnp.int32),
            vm((1, HD), jnp.int32),
            vm((SUB, 2, BLK, HD), BF16),
            vm((SUB, 1, HD), jnp.int32),
            vm((Z, 2, 2, HD), BF16),
            vm((2, GRP, 32, HD), BF16),
            vm((ALLR, HD), BF16),
            vm((ROWS, HD), F32),
            vm((ROWS, HD), F32),
            vm((ALLR, HD), BF16),
            vm((1, ALLR), F32),
            vm((KEYS, HD), BF16),
            vm((HD, KEYS), BF16),
            vm((KEYS, HD), F32),
            vm((BLK, HD), F32),
            vm((SUB, BLK, HD), F32),
            vm((SUB, BLK, HD), F32),
            vm((SUB, 1, ROWS), jnp.int32),
            vm((KEYS, ALLR), BF16),
            vm((KEYS, ALLR), BF16),
            vm((1, ALLR), F32),
            vm((HD, ALLR), F32),
            vm((ALLR, HD), BF16),
            vm((ALLR, HD), BF16),
            vm((16, HD), F32),
            vm((PROWS, HD), F32),
            vm((64, HD), F32),
            vm((SUB, 2, BLK, HD), BF16),
            vm((BLK, HD), F32),
            vm((BLK, HD), F32),
            vm((4, 2, BLK, HD), BF16),
            vm((3, 2, BLK, HD), BF16),
            vm((3, 2, BLK, HD), BF16),
            vm((GRP, 64, HD), BF16),
            vm((GRP, 64, HD), BF16),
            vm((Z, 2, 2, HD), BF16),
            vm((Z, 2, 2, HD), BF16),
            vm((Z, 2, HD), F32),
            vm((GRP * X, 2, HD), F32),
            dma((9,)),
            dma((1,)), dma((SUB, 2)),
            dma((1,)), dma((1,)),
            dma((1,)), dma((2,)),
            dma((2,)), dma((2,)),
            dma((1,)), dma((2,)),
            dma((1,)), dma((3, 2)),
            dma((1,)), dma((1,)),
            dma((1,)), dma((1,)),
            dma((1,)), dma((1,)),
            dma((1,)), dma((1,)),
        ],
        compiler_params=pltpu.CompilerParams(
            collective_id=0, has_side_effects=True, vmem_limit_bytes=60 * 1024 * 1024
        ),
        name="tree_back",
    )(
        branch_q[:, 0], branch_k[:, 0], branch_v[:, 0], branch_o[:, 0], branch_dout[:, 0],
        prompt_q[:, 0], prompt_k[:, 0], prompt_v[:, 0], prompt_o[:, 0], prompt_dout[:, 0],
        gains, parents.reshape(1, 1), depth.reshape(1, BLK),
        jnp.asarray(np.concatenate([offset, level, prompt], axis=1)),
    )
    outs = pl.pallas_call(
        finish,
        out_shape=tuple(jax.ShapeDtypeStruct(x.shape, x.dtype) for x in outs),
        in_specs=[vmem] * 7,
        out_specs=(vmem,) * 7,
        name="finish",
    )(*outs)
    dq, dk, dv, pdq, pdk, pdv, gain_grads = outs
    return (
        dq[:, None], dk[:, None], dv[:, None], pdq[:, None], pdk[:, None], pdv[:, None], gain_grads,
    )


def solution(mesh):
    tok = P("ctx", "head", None)
    return jax.shard_map(
        per_device,
        mesh=mesh,
        in_specs=(tok,) * 10 + (P(), P("ctx"), P("ctx")),
        out_specs=(tok,) * 6 + (P(),),
        check_vma=False,
    )
```
